32 devices in a mesh: gx: 4 (over z), gy: 4 (over y, x), gz: 2 (over core).
Axes of the slice: x: 2, y: 2, z: 4, core: 2. Of those that a mesh axis runs over, the one named last changes fastest.
Arguments:
- volume: float32 [9, 16, 256, 512], P(None, 'gz', 'gx', 'gy'), may hold values from -6 to 6
- materials: float32 [3, 16, 256, 512], P(None, 'gz', 'gx', 'gy'), may hold values from 0.4 to 1.2
- water_height: float32 [128, 4096], P(('gx', 'gy', 'gz')), may hold values from 2 to 4
- water_flow: float32 [2, 128, 4096], P(None, ('gx', 'gy', 'gz')), may hold values from -3 to 3
- owner_of: int32 [128], replicated, may hold values from 0 to 31, as said below
- patch_tile: int32 [128], replicated, may hold values from 0 to 511, as said below
Outputs:
- volume_next: float32 [9, 16, 256, 512], P(None, 'gz', 'gx', 'gy')
- water_next: float32 [3, 128, 4096], P(None, ('gx', 'gy', 'gz'))
The draws below stay inside these ranges and needn't reach their ends.
Inputs may be any that keep to these rules, and one draw needn't show every extreme that they name: `owner_of`: every device index owns exactly 4 patches, and the tiles of one owner's patches lie in the blocks of 4 different devices along gx and gy. `patch_tile`: all values are distinct; the block of each device along gx and gy holds the tiles of exactly 4 * (number of devices along gz) patches.
All inputs are finite; a program needn't handle non-finite values.
Results may differ from the reference program's by a relative error of at most 0.0001.
Values sent between devices are 32-bit elements; how exact they have to be, the bound alone decides.
A program may use at most 128 MiB of HBM per device.

```python
import jax
import jax.numpy as jnp

CX = 64
CY = 128
PATCH_DEV = 4
PS = 16
REFINE = 4
NX = 256
NY = 512
NZ = 16
FP = 64
NPATCH = 128


def joint_draw(key):
    tops_y = NY // CY
    tops = NX // CX * tops_y
    blocks_x = CX // PS
    blocks_y = CY // PS
    local_count = blocks_x * blocks_y
    slots = jnp.arange(NPATCH, dtype=jnp.int32)
    first_owner = slots // PATCH_DEV
    source = slots % tops
    place = slots // tops
    scores = jax.random.randint(jax.random.fold_in(key, 51), (tops, local_count), 0, 1 << 20) * local_count
    scores = scores + jnp.arange(local_count, dtype=jnp.int32)[None, :]
    scores = scores.at[0, 0].set(-1).at[tops - 1, local_count - 1].set(-1)
    table = jnp.argsort(scores, axis=1, stable=True).astype(jnp.int32)
    local = table[source, place]
    tile_x = source // tops_y * blocks_x + local // blocks_y
    tile_y = source % tops_y * blocks_y + local % blocks_y
    tile = (tile_x * (NY // PS) + tile_y).astype(jnp.int32)
    relabel = jax.random.permutation(jax.random.fold_in(key, 52), NPATCH // PATCH_DEV).astype(jnp.int32)
    owner = jnp.take(relabel, first_owner).astype(jnp.int32)
    mixing = jax.random.permutation(jax.random.fold_in(key, 53), NPATCH).astype(jnp.int32)
    owner_all = jnp.zeros((NPATCH,), jnp.int32).at[mixing].set(owner)
    tile_all = jnp.zeros((NPATCH,), jnp.int32).at[mixing].set(tile)
    return (owner_all, tile_all)


def draw_owner_of(key, part):
    return joint_draw(key)[0]


def draw_patch_tile(key, part):
    return joint_draw(key)[1]


def level_of(stream_key, shape, pieces, low, high):
    loudness, own = 1.0, jax.random.fold_in(stream_key, 6)
    for position, shards_of in pieces:
        heights = jnp.exp(jax.random.uniform(jax.random.fold_in(own, position), (shards_of,), jnp.float32, low / len(pieces), high / len(pieces)))
        loudness = loudness * jnp.repeat(heights, shape[position] // shards_of).reshape([-1 if axis == position else 1 for axis in range(len(shape))])
    return loudness


def bell_draw(own_key, extent, deviation, bound, shards=(), kind=jnp.bfloat16):
    entries = jax.random.normal(own_key, extent, jnp.float32) * deviation
    if len(shards) > 0:
        entries = level_of(own_key, extent, shards, -0.22, 0.18) * entries
    return jnp.clip(entries, min=-bound, max=bound).astype(kind)


def setup_inputs(seed: int = 0) -> dict:
    splits = jax.random.split(jax.random.key(seed), 7)
    volume = bell_draw(splits[0], (9, NZ, NX, NY), 1.0, 6.0, ((1, 2), (2, 4), (3, 4)), jnp.float32)
    materials = jnp.clip(0.4 + 0.800000042 * jax.random.uniform(splits[1], (3, NZ, NX, NY), jnp.float32) ** level_of(splits[1], (3, NZ, NX, NY), ((1, 2), (2, 4), (3, 4)), -0.2, 0.2), 0.4, 1.2)
    water_height = jnp.clip(2.0 + 2.0 * jax.random.uniform(splits[2], (NPATCH, FP * FP), jnp.float32) ** level_of(splits[2], (NPATCH, FP * FP), ((0, 32),), -0.2, 0.2), 2.0, 4.0)
    water_flow = bell_draw(splits[3], (2, NPATCH, FP * FP), 0.5, 3.0, ((1, 32),), jnp.float32)
    owner_of = draw_owner_of(jax.random.fold_in(splits[6], 71), 0)
    patch_tile = draw_patch_tile(jax.random.fold_in(splits[6], 71), 0)
    return dict(volume=volume, materials=materials, water_height=water_height, water_flow=water_flow, owner_of=owner_of, patch_tile=patch_tile)


wave_ratio = 0.075
flux_ratio = 0.05
uplift_rate = 1.0
gravity = 1.0


def elastic_step(padded, materials):
    def neighbours(field):
        return (padded[field, 2:, 1:-1, 1:-1], padded[field, :-2, 1:-1, 1:-1],
                padded[field, 1:-1, 2:, 1:-1], padded[field, 1:-1, :-2, 1:-1],
                padded[field, 1:-1, 1:-1, 2:], padded[field, 1:-1, 1:-1, :-2])

    def average(field):
        six = neighbours(field)
        return (six[0] + six[1] + six[2] + six[3] + six[4] + six[5]) / 6.0

    def across(field, along):
        six = neighbours(field)
        return six[2 * along] - six[2 * along + 1]

    buoyancy = materials[0]
    lame_first = materials[1]
    shear = materials[2]
    divergence = across(0, 1) + across(1, 2) + across(2, 0)
    rates = [
        buoyancy * (across(3, 1) + across(6, 2) + across(7, 0)),
        buoyancy * (across(6, 1) + across(4, 2) + across(8, 0)),
        buoyancy * (across(7, 1) + across(8, 2) + across(5, 0)),
        lame_first * divergence + 2.0 * shear * across(0, 1),
        lame_first * divergence + 2.0 * shear * across(1, 2),
        lame_first * divergence + 2.0 * shear * across(2, 0),
        shear * (across(0, 2) + across(1, 1)),
        shear * (across(0, 0) + across(2, 1)),
        shear * (across(1, 0) + across(2, 2)),
    ]
    return jnp.stack([average(field) + wave_ratio * rates[field] for field in range(9)])


def tile_blocks(layer):
    blocks_x = layer.shape[0] // PS
    blocks_y = layer.shape[1] // PS
    grid = layer.reshape(blocks_x, PS, blocks_y, PS).transpose(0, 2, 1, 3)
    return grid.reshape(blocks_x * blocks_y, PS * PS)


def refine(coarse):
    row_count = coarse.shape[0]
    grid = coarse.reshape(row_count, PS, 1, PS, 1)
    return jnp.broadcast_to(grid, (row_count, PS, REFINE, PS, REFINE)).reshape(row_count, FP * FP)


def edge_strips(state):
    strips = jnp.stack([state[:, :, 0, :], state[:, :, -1, :], state[:, :, :, 0], state[:, :, :, -1]], axis=0)
    return strips.transpose(2, 0, 1, 3).reshape(state.shape[1], 12 * FP)


def neighbour_rows(tiles_here, tile_row, tiles_x, tiles_y):
    tile_x = tiles_here // tiles_y
    tile_y = tiles_here % tiles_y
    wanted_list = [(tile_x > 0, tiles_here - tiles_y, 1), (tile_x < tiles_x - 1, tiles_here + tiles_y, 0),
                   (tile_y > 0, tiles_here - 1, 3), (tile_y < tiles_y - 1, tiles_here + 1, 2)]
    row_ids = jnp.arange(tile_row.shape[0], dtype=jnp.int32)
    links = []
    for valid, wanted, edge_id in wanted_list:
        match = tile_row[None, :] == wanted[:, None]
        found = valid & jnp.any(match, axis=1)
        other_row = jnp.sum(jnp.where(match, row_ids[None, :], 0), axis=1).astype(jnp.int32)
        links.append((found, other_row, edge_id))
    return links


def assemble(state, strips_all, links):
    owned = [state[:, :, 0, :], state[:, :, -1, :], state[:, :, :, 0], state[:, :, :, -1]]
    ghosts = []
    for side in range(4):
        found, other_row, edge_id = links[side]
        other = jnp.take(strips_all, other_row, axis=0)[:, edge_id].transpose(1, 0, 2)
        ghosts.append(jnp.where(found[None, :, None], other, owned[side]))
    extended = jnp.pad(state, ((0, 0), (0, 0), (1, 1), (1, 1)))
    extended = extended.at[:, :, 0, 1:-1].set(ghosts[0])
    extended = extended.at[:, :, -1, 1:-1].set(ghosts[1])
    extended = extended.at[:, :, 1:-1, 0].set(ghosts[2])
    extended = extended.at[:, :, 1:-1, -1].set(ghosts[3])
    return extended


def fluxes_x(part):
    height, flow_x, flow_y = part[0], part[1], part[2]
    speed = flow_x / height
    return jnp.stack([flow_x, flow_x * speed + 0.5 * gravity * height * height, flow_y * speed])


def fluxes_y(part):
    height, flow_x, flow_y = part[0], part[1], part[2]
    speed = flow_y / height
    return jnp.stack([flow_y, flow_x * speed, flow_y * speed + 0.5 * gravity * height * height])


def water_step(extended, lift):
    east = extended[:, :, 2:, 1:-1]
    west = extended[:, :, :-2, 1:-1]
    north = extended[:, :, 1:-1, 2:]
    south = extended[:, :, 1:-1, :-2]
    updated = 0.25 * (east + west + north + south) - flux_ratio * (
        (fluxes_x(east) - fluxes_x(west)) + (fluxes_y(north) - fluxes_y(south)))
    patches = extended.shape[1]
    updated = updated.at[0].add(uplift_rate * lift.reshape(patches, FP, FP))
    return updated.reshape(3, patches, FP * FP)


def reference(volume, materials, water_height, water_flow, owner_of, patch_tile):
    padded = jnp.pad(volume, ((0, 0), (1, 1), (1, 1), (1, 1)))
    volume_next = elastic_step(padded, materials)
    order = jnp.argsort(owner_of, stable=True).astype(jnp.int32)
    tile_row = jnp.take(patch_tile, order).astype(jnp.int32)
    tiles_all = tile_blocks(volume_next[2, 0])
    lift = refine(jnp.take(tiles_all, tile_row, axis=0))
    state = jnp.concatenate([water_height[None], water_flow], axis=0).reshape(3, NPATCH, FP, FP)
    strips_all = edge_strips(state).reshape(NPATCH, 4, 3, FP)
    links = neighbour_rows(tile_row, tile_row, NX // PS, NY // PS)
    extended = assemble(state, strips_all, links)
    return volume_next, water_step(extended, lift)
```

```python
import functools

import jax
import jax.numpy as jnp
from jax import lax
from jax.experimental import pallas as pl
from jax.experimental.pallas import tpu as pltpu
from jax.sharding import PartitionSpec as P

PATCH_DEV = 4
PS = 16
REFINE = 4
FP = 64
LANES = 128
MESH = pl.DeviceIdType.MESH

wave_ratio = 0.075
flux_ratio = 0.05
uplift_rate = 1.0
gravity = 1.0


def log2(n):
    assert n & (n - 1) == 0
    return n.bit_length() - 1


def iota(shape, dim):
    return lax.broadcasted_iota(jnp.int32, shape, dim)


def exact_dot(a, b):
    return jnp.dot(a, b, precision=lax.Precision.HIGHEST, preferred_element_type=jnp.float32)


def pick_sum(mask, values):
    picked = jnp.where(mask, values.astype(jnp.float32), 0.0)
    return jnp.sum(picked, axis=1, keepdims=True).astype(jnp.int32)


def six_neighbours(ext, yl, yr, f, z, z_index, rows, row0, depth):
    lane = iota((rows, LANES), 1)
    at = f * depth + z
    top = row0 + 8
    mid = ext[f, z_index, top : top + rows, :]
    left = jnp.where(
        lane == 0,
        pltpu.roll(yl[row0 : row0 + rows, :], (LANES - at) & (LANES - 1), 1),
        pltpu.roll(mid, 1, 1),
    )
    right = jnp.where(
        lane == LANES - 1,
        pltpu.roll(yr[row0 : row0 + rows, :], LANES - 1 - at, 1),
        pltpu.roll(mid, LANES - 1, 1),
    )
    return (
        ext[f, z_index + 1, top : top + rows, :],
        ext[f, z_index - 1, top : top + rows, :],
        ext[f, z_index, top + 1 : top + 1 + rows, :],
        ext[f, z_index, top - 1 : top - 1 + rows, :],
        right,
        left,
    )


def mean_of(six):
    return (six[0] + six[1] + six[2] + six[3] + six[4] + six[5]) * (1.0 / 6.0)


def kernel(
    sizes,
    own_ref, til_ref, h_ref, fl_ref, vol_hbm, mat_hbm,
    vout_hbm, wout_ref,
    ext, mat, outv, ys_lo, ys_hi, yl, yr, strips, slots, lifts,
    vol_sem, mat_sem, out_sem, halo_send, halo_recv, st_send, st_recv, sib_send, sib_recv,
    lift_send, lift_recv,
):
    ngx, ngy, ngz, patches, depth, cx = sizes
    ndev = ngx * ngy * ngz
    nblk = ngx * ngy
    gx, gy, gz = lax.axis_index("gx"), lax.axis_index("gy"), lax.axis_index("gz")
    blk = gx * ngy + gy
    me = blk * ngz + gz
    local_x, local_y = cx // PS, LANES // PS
    tiles_x, tiles_y = local_x * ngx, local_y * ngy

    def coords(d):
        return (d // (ngy * ngz), (d // ngz) % ngy, d % ngz)

    vol_copy = pltpu.make_async_copy(
        vol_hbm, ext.at[:, pl.ds(1, depth), pl.ds(8, cx), :], vol_sem
    )
    vol_copy.start()
    mat_copy = pltpu.make_async_copy(mat_hbm, mat, mat_sem)
    mat_copy.start()

    barrier = pltpu.get_barrier_semaphore()

    def greet(i, carry):
        pl.semaphore_signal(
            barrier, inc=1, device_id=coords((me + i) % ndev), device_id_type=MESH
        )
        return carry

    lax.fori_loop(1, ndev, greet, 0)

    @pl.when(gz == 0)
    def _():
        ext[:, 0] = jnp.zeros_like(ext[:, 0])

    @pl.when(gz == ngz - 1)
    def _():
        ext[:, depth + 1] = jnp.zeros_like(ext[:, depth + 1])

    @pl.when(gx == 0)
    def _():
        ext[:, 1 : depth + 1, 7:8, :] = jnp.zeros((9, depth, 1, LANES), jnp.float32)

    @pl.when(gx == ngx - 1)
    def _():
        ext[:, 1 : depth + 1, cx + 8 : cx + 9, :] = jnp.zeros((9, depth, 1, LANES), jnp.float32)

    @pl.when(gy == 0)
    def _():
        yl[...] = jnp.zeros_like(yl)

    @pl.when(gy == ngy - 1)
    def _():
        yr[...] = jnp.zeros_like(yr)

    lane4 = iota((PATCH_DEV, LANES), 1)
    half = lane4 & (FP - 1)
    state = [h_ref[...], fl_ref[0], fl_ref[1]]
    groups = FP * FP // LANES
    for c in range(3):
        st = state[c]
        strips[gz, blk, 4 * c : 4 * c + 4, :] = jnp.where(
            lane4 < FP, st[:, :LANES], st[:, FP * FP - LANES :]
        )
        packed = jnp.zeros((PATCH_DEV, LANES), jnp.float32)
        for k in range(groups):
            part = st[:, LANES * k : LANES * (k + 1)]
            first = part if k == 0 else pltpu.roll(part, k, 1)
            packed = jnp.where(half == k, first, packed)
            packed = jnp.where(half == 32 + k, pltpu.roll(part, (k + 97) % LANES, 1), packed)
        strips[gz, blk, 12 + 4 * c : 16 + 4 * c, :] = packed

    vol_copy.wait()

    lane_c = iota((cx, LANES), 1)

    def pack(z, carry):
        lo, hi = carry
        for f in range(9):
            at = f * depth + z
            u = ext[f, z + 1, 8 : 8 + cx, :]
            lo = jnp.where(lane_c == at, pltpu.roll(u, at, 1), lo)
            hi = jnp.where(lane_c == at, pltpu.roll(u, at + 1, 1), hi)
        return lo, hi

    zero_face = jnp.zeros((cx, LANES), jnp.float32)
    lo, hi = lax.fori_loop(0, depth, pack, (zero_face, zero_face))
    ys_lo[...] = lo
    ys_hi[...] = hi

    pl.semaphore_wait(barrier, ndev - 1)

    def remote(src, dst, k, target):
        return pltpu.make_async_remote_copy(
            src_ref=src, dst_ref=dst, send_sem=halo_send.at[k], recv_sem=halo_recv.at[k],
            device_id=target, device_id_type=MESH,
        )

    inner = pl.ds(1, depth)
    halos = [
        (gy < ngy - 1, gy > 0, remote(ys_hi, yl, 0, (gx, gy + 1, gz))),
        (gy > 0, gy < ngy - 1, remote(ys_lo, yr, 1, (gx, gy - 1, gz))),
        (gx < ngx - 1, gx > 0, remote(
            ext.at[:, inner, pl.ds(cx + 7, 1), :], ext.at[:, inner, pl.ds(7, 1), :],
            2, (gx + 1, gy, gz))),
        (gx > 0, gx < ngx - 1, remote(
            ext.at[:, inner, pl.ds(8, 1), :], ext.at[:, inner, pl.ds(cx + 8, 1), :],
            3, (gx - 1, gy, gz))),
        (gz < ngz - 1, gz > 0, remote(
            ext.at[:, depth, pl.ds(8, cx), :], ext.at[:, 0, pl.ds(8, cx), :],
            4, (gx, gy, gz + 1))),
        (gz > 0, gz < ngz - 1, remote(
            ext.at[:, 1, pl.ds(8, cx), :], ext.at[:, depth + 1, pl.ds(8, cx), :],
            5, (gx, gy, gz - 1))),
    ]
    for has_target, _, copy in halos:
        pl.when(has_target)(copy.start)

    def spread(i, carry):
        b = (blk + i) % nblk
        pltpu.make_async_remote_copy(
            src_ref=strips.at[gz, blk], dst_ref=strips.at[gz, blk],
            send_sem=st_send, recv_sem=st_recv,
            device_id=(b // ngy, b % ngy, gz), device_id_type=MESH,
        ).start()
        return carry

    lax.fori_loop(1, nblk, spread, 0)

    owner = own_ref[...]
    tile = til_ref[...]
    square = (patches, patches)
    owner_wide = jnp.broadcast_to(owner, square)
    owner_col = pick_sum(iota(square, 0) == iota(square, 1), owner_wide)
    earlier = (owner_col == owner_wide) & (iota(square, 0) < iota(square, 1))
    rank = jnp.sum(jnp.where(earlier, 1.0, 0.0), axis=0, keepdims=True).astype(jnp.int32)
    row_of = owner * PATCH_DEV + rank
    tile_x = tile >> log2(tiles_y)
    tile_y = tile & (tiles_y - 1)
    wide8 = (8, patches)
    row_of8 = jnp.broadcast_to(row_of, wide8)
    tile8 = jnp.broadcast_to(tile, wide8)
    mine = row_of8 == me * PATCH_DEV + iota(wide8, 0)
    mine = mine & (iota(wide8, 0) < PATCH_DEV)
    my_tile = pick_sum(mine, tile8)
    my_x = my_tile >> log2(tiles_y)
    my_y = my_tile & (tiles_y - 1)
    my_blk = (my_x >> log2(local_x)) * ngy + (my_y >> log2(local_y))

    founds = []
    picks = []
    keys = (8, ndev * 24)
    for side, (valid, want) in enumerate(
        [
            (my_x > 0, my_tile - tiles_y),
            (my_x < tiles_x - 1, my_tile + tiles_y),
            (my_y > 0, my_tile - 1),
            (my_y < tiles_y - 1, my_tile + 1),
        ]
    ):
        match = tile8 == jnp.where(valid, want, -1)
        other = pick_sum(match, row_of8 + 1) - 1
        founds.append((other >= 0)[:PATCH_DEV])
        dev = other >> log2(PATCH_DEV)
        place = (dev & (ngz - 1)) * nblk + (dev >> log2(ngz))
        target = place * 24 + (other & (PATCH_DEV - 1))
        for c in range(3):
            q = c if side < 2 else 3 + c
            goal = jnp.where(other >= 0, target + 4 * q, -1)
            picks.append(jnp.where(iota(keys, 1) == goal, 1.0, 0.0))
    pick_all = jnp.concatenate(picks, axis=0)

    for k in range(4):
        pl.when(halos[k][1])(halos[k][2].wait_recv)
    mat_copy.wait()

    @pl.when(gz == 0)
    def _():
        def diff(f, along):
            six = six_neighbours(ext, yl, yr, f, 0, 1, cx, 0, depth)
            return six[2 * along] - six[2 * along + 1]

        def vz_sum():
            six = six_neighbours(ext, yl, yr, 2, 0, 1, cx, 0, depth)
            return mean_of(six)

        rate = mat[0, 0] * (diff(7, 1) + diff(8, 2) + diff(5, 0))
        floor = vz_sum() + wave_ratio * rate

        tall = (ndev * PS, patches)
        here = (
            (tile_x >> log2(local_x) == gx) & (tile_y >> log2(local_y) == gy)
        )
        owner_here = jnp.where(here, owner, -1)
        chosen = jnp.broadcast_to(owner_here, tall) == (iota(tall, 0) >> log2(PS))
        local = (tile_x & (local_x - 1)) * local_y + (tile_y & (local_y - 1)) + 1
        local_col = pick_sum(chosen, jnp.broadcast_to(local, tall)) - 1
        local_tx = local_col >> log2(local_y)
        local_ty = local_col & (local_y - 1)
        wide = (ndev * PS, cx)
        row_want = local_tx * PS + (iota((ndev * PS, 1), 0) & (PS - 1))
        band = exact_dot(jnp.where(iota(wide, 1) == row_want, 1.0, 0.0), floor)
        full = (ndev * PS, LANES)
        band = jnp.where((iota(full, 1) >> log2(PS)) == local_ty, band, 0.0)
        same = (iota((LANES, LANES), 0) & (PS - 1)) == (iota((LANES, LANES), 1) & (PS - 1))
        spread_lanes = exact_dot(band, jnp.where(same, 1.0, 0.0))
        kept = jnp.where(
            (iota(full, 1) >> log2(PS)) == (iota(full, 0) & 7), spread_lanes, 0.0
        )
        rows = jnp.sum(kept.reshape(ndev * 2, 8, LANES), axis=1)
        for d in range(ndev):
            slots[d] = rows[2 * d : 2 * d + 2, :]

        def send_lift(i, carry):
            d = (me + i) % ndev
            pltpu.make_async_remote_copy(
                src_ref=slots.at[d], dst_ref=lifts.at[blk],
                send_sem=lift_send, recv_sem=lift_recv,
                device_id=coords(d), device_id_type=MESH,
            ).start()
            return carry

        lax.fori_loop(1, ndev, send_lift, 0)
        lifts[blk] = slots[me]

    for k in range(4, 6):
        pl.when(halos[k][1])(halos[k][2].wait_recv)

    def layer(z, carry):
        for row0 in range(0, cx, 16):
            sixes = {}

            def six(f):
                if f not in sixes:
                    sixes[f] = six_neighbours(ext, yl, yr, f, z, z + 1, 16, row0, depth)
                return sixes[f]

            def across(f, along):
                return six(f)[2 * along] - six(f)[2 * along + 1]

            def put(f, rate):
                outv[f, z, row0 : row0 + 16, :] = mean_of(six(f)) + wave_ratio * rate

            buoyancy = mat[0, z, row0 : row0 + 16, :]
            lame = mat[1, z, row0 : row0 + 16, :]
            shear = mat[2, z, row0 : row0 + 16, :]
            dx, dy, dz = across(0, 1), across(1, 2), across(2, 0)
            ldiv = lame * (dx + dy + dz)
            put(0, buoyancy * (across(3, 1) + across(6, 2) + across(7, 0)))
            put(1, buoyancy * (across(6, 1) + across(4, 2) + across(8, 0)))
            put(2, buoyancy * (across(7, 1) + across(8, 2) + across(5, 0)))
            put(3, ldiv + 2.0 * shear * dx)
            put(4, ldiv + 2.0 * shear * dy)
            put(5, ldiv + 2.0 * shear * dz)
            put(6, shear * (across(0, 2) + across(1, 1)))
            put(7, shear * (across(0, 0) + across(2, 1)))
            put(8, shear * (across(1, 0) + across(2, 2)))
        return carry

    def store_layers(start, count, k):
        return pltpu.make_async_copy(
            outv.at[:, pl.ds(start, count)], vout_hbm.at[:, pl.ds(start, count)], out_sem.at[k]
        )

    first_part = depth // 2
    lax.fori_loop(0, first_part, layer, 0)
    store_a = store_layers(0, first_part, 0)
    store_a.start()

    some = strips.at[gz, pl.ds(0, nblk - 1)]
    pltpu.make_async_copy(some, some, st_recv).wait()

    def hand(i):
        other = (gz + i) % ngz
        return pltpu.make_async_remote_copy(
            src_ref=strips.at[gz], dst_ref=strips.at[gz],
            send_sem=sib_send.at[i - 1], recv_sem=sib_recv.at[i - 1],
            device_id=(gx, gy, other), device_id_type=MESH,
        )

    for i in range(1, ngz):
        hand(i).start()
    lax.fori_loop(first_part, depth, layer, 0)
    store_b = store_layers(first_part, depth - first_part, 1)
    store_b.start()

    for i in range(1, ngz):
        hand(i).wait_recv()
    ghosts = exact_dot(pick_all, strips[...].reshape(ndev * 24, LANES))

    @pl.when(gz == 0)
    def _():
        part = lifts.at[pl.ds(0, nblk - 1)]
        pltpu.make_async_copy(part, part, lift_recv).wait()

    @pl.when(gz != 0)
    def _():
        pltpu.make_async_copy(lifts, lifts, lift_recv).wait()

    chooser = jnp.where(iota((8, nblk), 1) == my_blk, 1.0, 0.0)
    coarse = [exact_dot(chooser, lifts[:, k, :]) for k in range(2)]
    wide_lane = iota((LANES, 8 * LANES), 1)
    source = (wide_lane >> log2(LANES)) * PS + ((wide_lane & (FP - 1)) >> log2(REFINE))
    expand = jnp.where(iota((LANES, 8 * LANES), 0) == source, 1.0, 0.0)
    fine = [exact_dot(coarse[k], expand)[:PATCH_DEV] for k in range(2)]
    lift = jnp.concatenate(
        [
            fine[(k // 2) // 8][:, LANES * ((k // 2) % 8) : LANES * ((k // 2) % 8 + 1)]
            for k in range(groups)
        ],
        axis=1,
    )

    lane = iota((PATCH_DEV, FP * FP), 1)
    col = lane & (FP - 1)

    def ghost(side, c):
        at = (side * 3 + c) * 8
        return ghosts[at : at + PATCH_DEV, :]

    def beside(c, side):
        st = state[c]
        g = ghost(side, c)
        if side == 0:
            wide = jnp.concatenate([pltpu.roll(g, FP, 1)] * groups, axis=1)
            edge, moved = lane < FP, pltpu.roll(st, FP, 1)
        elif side == 1:
            wide = jnp.concatenate([pltpu.roll(g, FP, 1)] * groups, axis=1)
            edge, moved = lane >= FP * FP - FP, pltpu.roll(st, FP * FP - FP, 1)
        elif side == 2:
            wide = jnp.concatenate([pltpu.roll(g, 96 - k, 1) for k in range(groups)], axis=1)
            edge, moved = col == 0, pltpu.roll(st, 1, 1)
        else:
            wide = jnp.concatenate([pltpu.roll(g, 63 - k, 1) for k in range(groups)], axis=1)
            edge, moved = col == FP - 1, pltpu.roll(st, FP * FP - 1, 1)
        return jnp.where(edge, jnp.where(founds[side], wide, st), moved)

    sides = [[beside(c, side) for c in range(3)] for side in range(4)]

    def fluxes_x(part):
        height, flow_x, flow_y = part
        speed = flow_x / height
        return [flow_x, flow_x * speed + 0.5 * gravity * height * height, flow_y * speed]

    def fluxes_y(part):
        height, flow_x, flow_y = part
        speed = flow_y / height
        return [flow_y, flow_x * speed, flow_y * speed + 0.5 * gravity * height * height]

    fw, fe = fluxes_x(sides[0]), fluxes_x(sides[1])
    fs, fn = fluxes_y(sides[2]), fluxes_y(sides[3])
    for c in range(3):
        updated = 0.25 * (sides[1][c] + sides[0][c] + sides[3][c] + sides[2][c]) - flux_ratio * (
            (fe[c] - fw[c]) + (fn[c] - fs[c])
        )
        if c == 0:
            updated = updated + uplift_rate * lift
        wout_ref[c] = updated

    store_a.wait()
    store_b.wait()
    for has_target, _, copy in halos:
        pl.when(has_target)(copy.wait_send)
    pltpu.make_async_copy(some, some, st_send).wait()
    for i in range(1, ngz):
        hand(i).wait_send()

    @pl.when(gz == 0)
    def _():
        sent = slots.at[pl.ds(0, ndev - 1)]
        pltpu.make_async_copy(sent, sent, lift_send).wait()


def per_device(volume, materials, water_height, water_flow, owner_of, patch_tile):
    ngx, ngy, ngz = (lax.axis_size(a) for a in ("gx", "gy", "gz"))
    ndev, nblk = ngx * ngy * ngz, ngx * ngy
    fields, depth, cx, cy = volume.shape
    patches = owner_of.shape[0]
    assert cy == LANES and fields * depth <= LANES
    f32 = jnp.float32
    dma = pltpu.SemaphoreType.DMA
    vmem = pl.BlockSpec(memory_space=pltpu.VMEM)
    anywhere = pl.BlockSpec(memory_space=pl.ANY)
    return pl.pallas_call(
        functools.partial(kernel, (ngx, ngy, ngz, patches, depth, cx)),
        name="coupled_step",
        out_shape=(
            jax.ShapeDtypeStruct(volume.shape, f32),
            jax.ShapeDtypeStruct((3,) + water_height.shape, f32),
        ),
        in_specs=[vmem, vmem, vmem, vmem, anywhere, anywhere],
        out_specs=(anywhere, vmem),
        scratch_shapes=[
            pltpu.VMEM((fields, depth + 2, cx + 16, LANES), f32),
            pltpu.VMEM(materials.shape, f32),
            pltpu.VMEM(volume.shape, f32),
            pltpu.VMEM((cx, LANES), f32),
            pltpu.VMEM((cx, LANES), f32),
            pltpu.VMEM((cx, LANES), f32),
            pltpu.VMEM((cx, LANES), f32),
            pltpu.VMEM((ngz, nblk, 24, LANES), f32),
            pltpu.VMEM((ndev, 2, LANES), f32),
            pltpu.VMEM((nblk, 2, LANES), f32),
            dma, dma, dma((2,)), dma((6,)), dma((6,)), dma, dma,
            dma((max(ngz - 1, 1),)), dma((max(ngz - 1, 1),)), dma, dma,
        ],
        compiler_params=pltpu.CompilerParams(collective_id=0, has_side_effects=True, vmem_limit_bytes=56 * 1024 * 1024),
    )(
        owner_of.reshape(1, patches), patch_tile.reshape(1, patches),
        water_height, water_flow, volume, materials,
    )


def solution(mesh):
    return jax.shard_map(
        per_device,
        mesh=mesh,
        in_specs=(
            P(None, "gz", "gx", "gy"),
            P(None, "gz", "gx", "gy"),
            P(("gx", "gy", "gz"), None),
            P(None, ("gx", "gy", "gz"), None),
            P(),
            P(),
        ),
        out_specs=(P(None, "gz", "gx", "gy"), P(None, ("gx", "gy", "gz"), None)),
        check_vma=False,
    )
```

```python
import functools

import jax
import jax.numpy as jnp
from jax import lax
from jax.experimental import pallas as pl
from jax.experimental.pallas import tpu as pltpu
from jax.sharding import PartitionSpec as P

PATCH_DEV = 4
PS = 16
REFINE = 4
FP = 64
LANES = 128
MESH = pl.DeviceIdType.MESH

wave_ratio = 0.075
flux_ratio = 0.05
uplift_rate = 1.0
gravity = 1.0


def log2(n):
    assert n & (n - 1) == 0
    return n.bit_length() - 1


def iota(shape, dim):
    return lax.broadcasted_iota(jnp.int32, shape, dim)


def exact_dot(a, b):
    return jnp.dot(a, b, precision=lax.Precision.HIGHEST, preferred_element_type=jnp.float32)


def pick_sum(mask, values):
    picked = jnp.where(mask, values.astype(jnp.float32), 0.0)
    return jnp.sum(picked, axis=1, keepdims=True).astype(jnp.int32)


def six_neighbours(ext, yl, yr, f, z, z_index, rows, row0, depth):
    lane = iota((rows, LANES), 1)
    at = f * depth + z
    top = row0 + 8
    mid = ext[f, z_index, top : top + rows, :]
    left = jnp.where(
        lane == 0,
        pltpu.roll(yl[row0 : row0 + rows, :], (LANES - at) & (LANES - 1), 1),
        pltpu.roll(mid, 1, 1),
    )
    right = jnp.where(
        lane == LANES - 1,
        pltpu.roll(yr[row0 : row0 + rows, :], LANES - 1 - at, 1),
        pltpu.roll(mid, LANES - 1, 1),
    )
    return (
        ext[f, z_index + 1, top : top + rows, :],
        ext[f, z_index - 1, top : top + rows, :],
        ext[f, z_index, top + 1 : top + 1 + rows, :],
        ext[f, z_index, top - 1 : top - 1 + rows, :],
        right,
        left,
    )


def mean_of(six):
    return (six[0] + six[1] + six[2] + six[3] + six[4] + six[5]) * (1.0 / 6.0)


def kernel(
    sizes,
    own_hbm, til_hbm, h_hbm, fl_hbm, vol_hbm, mat_hbm,
    outv, state_out, ghosts_out, found_out, coarse_out,
    ext, mat, ys_lo, ys_hi, yl, yr, strips, slots, lifts,
    own_ref, til_ref, vol_sem, mat_sem, in_sem, halo_send, halo_recv, st_send, st_recv, sib_send, sib_recv,
    lift_send, lift_recv,
):
    ngx, ngy, ngz, patches, depth, cx = sizes
    ndev = ngx * ngy * ngz
    nblk = ngx * ngy
    gx, gy, gz = lax.axis_index("gx"), lax.axis_index("gy"), lax.axis_index("gz")
    blk = gx * ngy + gy
    me = blk * ngz + gz
    local_x, local_y = cx // PS, LANES // PS
    tiles_x, tiles_y = local_x * ngx, local_y * ngy

    def coords(d):
        return (d // (ngy * ngz), (d // ngz) % ngy, d % ngz)

    vol_copy = pltpu.make_async_copy(
        vol_hbm, ext.at[:, pl.ds(1, depth), pl.ds(8, cx), :], vol_sem
    )
    ins = [
        pltpu.make_async_copy(h_hbm, state_out.at[0], in_sem.at[0]),
        pltpu.make_async_copy(fl_hbm, state_out.at[pl.ds(1, 2)], in_sem.at[1]),
        pltpu.make_async_copy(own_hbm, own_ref, in_sem.at[2]),
        pltpu.make_async_copy(til_hbm, til_ref, in_sem.at[3]),
    ]
    for copy in ins:
        copy.start()
    vol_copy.start()
    mat_copy = pltpu.make_async_copy(mat_hbm, mat, mat_sem)
    mat_copy.start()

    barrier = pltpu.get_barrier_semaphore()

    def greet(i, carry):
        pl.semaphore_signal(
            barrier, inc=1, device_id=coords((me + i) % ndev), device_id_type=MESH
        )
        return carry

    lax.fori_loop(1, ndev, greet, 0)

    @pl.when(gz == 0)
    def _():
        ext[:, 0] = jnp.zeros_like(ext[:, 0])

    @pl.when(gz == ngz - 1)
    def _():
        ext[:, depth + 1] = jnp.zeros_like(ext[:, depth + 1])

    @pl.when(gx == 0)
    def _():
        ext[:, 1 : depth + 1, 7:8, :] = jnp.zeros((9, depth, 1, LANES), jnp.float32)

    @pl.when(gx == ngx - 1)
    def _():
        ext[:, 1 : depth + 1, cx + 8 : cx + 9, :] = jnp.zeros((9, depth, 1, LANES), jnp.float32)

    @pl.when(gy == 0)
    def _():
        yl[...] = jnp.zeros_like(yl)

    @pl.when(gy == ngy - 1)
    def _():
        yr[...] = jnp.zeros_like(yr)

    lane4 = iota((PATCH_DEV, LANES), 1)
    half = lane4 & (FP - 1)
    for copy in ins:
        copy.wait()
    state = [state_out[0], state_out[1], state_out[2]]
    groups = FP * FP // LANES
    for c in range(3):
        st = state[c]
        strips[gz, blk, 4 * c : 4 * c + 4, :] = jnp.where(
            lane4 < FP, st[:, :LANES], st[:, FP * FP - LANES :]
        )
        packed = jnp.zeros((PATCH_DEV, LANES), jnp.float32)
        for k in range(groups):
            part = st[:, LANES * k : LANES * (k + 1)]
            first = part if k == 0 else pltpu.roll(part, k, 1)
            packed = jnp.where(half == k, first, packed)
            packed = jnp.where(half == 32 + k, pltpu.roll(part, (k + 97) % LANES, 1), packed)
        strips[gz, blk, 12 + 4 * c : 16 + 4 * c, :] = packed

    vol_copy.wait()

    lane_c = iota((cx, LANES), 1)

    def pack(z, carry):
        lo, hi = carry
        for f in range(9):
            at = f * depth + z
            u = ext[f, z + 1, 8 : 8 + cx, :]
            lo = jnp.where(lane_c == at, pltpu.roll(u, at, 1), lo)
            hi = jnp.where(lane_c == at, pltpu.roll(u, at + 1, 1), hi)
        return lo, hi

    zero_face = jnp.zeros((cx, LANES), jnp.float32)
    lo, hi = lax.fori_loop(0, depth, pack, (zero_face, zero_face))
    ys_lo[...] = lo
    ys_hi[...] = hi

    pl.semaphore_wait(barrier, ndev - 1)

    def remote(src, dst, k, target):
        return pltpu.make_async_remote_copy(
            src_ref=src, dst_ref=dst, send_sem=halo_send.at[k], recv_sem=halo_recv.at[k],
            device_id=target, device_id_type=MESH,
        )

    inner = pl.ds(1, depth)
    halos = [
        (gy < ngy - 1, gy > 0, remote(ys_hi, yl, 0, (gx, gy + 1, gz))),
        (gy > 0, gy < ngy - 1, remote(ys_lo, yr, 1, (gx, gy - 1, gz))),
        (gx < ngx - 1, gx > 0, remote(
            ext.at[:, inner, pl.ds(cx + 7, 1), :], ext.at[:, inner, pl.ds(7, 1), :],
            2, (gx + 1, gy, gz))),
        (gx > 0, gx < ngx - 1, remote(
            ext.at[:, inner, pl.ds(8, 1), :], ext.at[:, inner, pl.ds(cx + 8, 1), :],
            3, (gx - 1, gy, gz))),
        (gz < ngz - 1, gz > 0, remote(
            ext.at[:, depth, pl.ds(8, cx), :], ext.at[:, 0, pl.ds(8, cx), :],
            4, (gx, gy, gz + 1))),
        (gz > 0, gz < ngz - 1, remote(
            ext.at[:, 1, pl.ds(8, cx), :], ext.at[:, depth + 1, pl.ds(8, cx), :],
            5, (gx, gy, gz - 1))),
    ]
    for has_target, _, copy in halos:
        pl.when(has_target)(copy.start)

    def spread(i, carry):
        b = (blk + i) % nblk
        pltpu.make_async_remote_copy(
            src_ref=strips.at[gz, blk], dst_ref=strips.at[gz, blk],
            send_sem=st_send, recv_sem=st_recv,
            device_id=(b // ngy, b % ngy, gz), device_id_type=MESH,
        ).start()
        return carry

    lax.fori_loop(1, nblk, spread, 0)

    owner = own_ref[...]
    tile = til_ref[...]
    square = (patches, patches)
    owner_wide = jnp.broadcast_to(owner, square)
    owner_col = pick_sum(iota(square, 0) == iota(square, 1), owner_wide)
    earlier = (owner_col == owner_wide) & (iota(square, 0) < iota(square, 1))
    rank = jnp.sum(jnp.where(earlier, 1.0, 0.0), axis=0, keepdims=True).astype(jnp.int32)
    row_of = owner * PATCH_DEV + rank
    tile_x = tile >> log2(tiles_y)
    tile_y = tile & (tiles_y - 1)
    wide8 = (8, patches)
    row_of8 = jnp.broadcast_to(row_of, wide8)
    tile8 = jnp.broadcast_to(tile, wide8)
    mine = row_of8 == me * PATCH_DEV + iota(wide8, 0)
    mine = mine & (iota(wide8, 0) < PATCH_DEV)
    my_tile = pick_sum(mine, tile8)
    my_x = my_tile >> log2(tiles_y)
    my_y = my_tile & (tiles_y - 1)
    my_blk = (my_x >> log2(local_x)) * ngy + (my_y >> log2(local_y))

    picks = []
    keys = (8, ndev * 24)
    for side, (valid, want) in enumerate(
        [
            (my_x > 0, my_tile - tiles_y),
            (my_x < tiles_x - 1, my_tile + tiles_y),
            (my_y > 0, my_tile - 1),
            (my_y < tiles_y - 1, my_tile + 1),
        ]
    ):
        match = tile8 == jnp.where(valid, want, -1)
        other = pick_sum(match, row_of8 + 1) - 1
        found_out[side] = jnp.broadcast_to(jnp.where(other >= 0, 1.0, 0.0), (8, LANES))
        dev = other >> log2(PATCH_DEV)
        place = (dev & (ngz - 1)) * nblk + (dev >> log2(ngz))
        target = place * 24 + (other & (PATCH_DEV - 1))
        for c in range(3):
            q = c if side < 2 else 3 + c
            goal = jnp.where(other >= 0, target + 4 * q, -1)
            picks.append(jnp.where(iota(keys, 1) == goal, 1.0, 0.0))
    pick_all = jnp.concatenate(picks, axis=0)

    chooser = jnp.where(iota((8, nblk), 1) == my_blk, 1.0, 0.0)
    here = (tile_x >> log2(local_x) == gx) & (tile_y >> log2(local_y) == gy)
    here_wide = jnp.broadcast_to(jnp.where(here, 1, 0), square)
    here_col = pick_sum(iota(square, 0) == iota(square, 1), here_wide)
    before = (here_col == 1) & (iota(square, 0) < iota(square, 1))
    place_row = jnp.sum(jnp.where(before, 1.0, 0.0), axis=0, keepdims=True).astype(jnp.int32)
    place_row = jnp.where(here, place_row, -1)
    count = PATCH_DEV * ngz
    tall = (count * PS, patches)
    chosen = jnp.broadcast_to(place_row, tall) == (iota(tall, 0) >> log2(PS))
    local = (tile_x & (local_x - 1)) * local_y + (tile_y & (local_y - 1)) + 1
    local_col = pick_sum(chosen, jnp.broadcast_to(local, tall)) - 1
    local_tx = local_col >> log2(local_y)
    local_ty = local_col & (local_y - 1)
    row_want = local_tx * PS + (iota((count * PS, 1), 0) & (PS - 1))
    row_pick = jnp.where(iota((count * PS, cx), 1) == row_want, 1.0, 0.0)
    full = (count * PS, LANES)
    lane_pick = (iota(full, 1) >> log2(PS)) == local_ty
    owner_here = jnp.where(here, owner, -1)
    slot_wide = (2 * ndev, patches)
    owned = jnp.broadcast_to(owner_here, slot_wide) == (iota(slot_wide, 0) >> 1)
    slot_place = pick_sum(owned, jnp.broadcast_to(place_row + 1, slot_wide)) - 1
    slot_row = jnp.where(slot_place >= 0, 2 * slot_place + (iota((2 * ndev, 1), 0) & 1), -1)
    slot_pick = jnp.where(iota((2 * ndev, 2 * count), 1) == slot_row, 1.0, 0.0)

    for k in range(4):
        pl.when(halos[k][1])(halos[k][2].wait_recv)
    mat_copy.wait()

    @pl.when(gz == 0)
    def _():
        def six(f):
            return six_neighbours(ext, yl, yr, f, 0, 1, cx, 0, depth)

        vz = six(2)
        sxz, syz = six(7), six(8)
        szz = ext[5, 2, 8 : 8 + cx, :] - ext[5, 0, 8 : 8 + cx, :]
        rate = mat[0, 0] * ((sxz[2] - sxz[3]) + (syz[4] - syz[5]) + szz)
        floor = mean_of(vz) + wave_ratio * rate
        band = jnp.where(lane_pick, exact_dot(row_pick, floor), 0.0)
        same = (iota((LANES, LANES), 0) & (PS - 1)) == (iota((LANES, LANES), 1) & (PS - 1))
        spread_lanes = exact_dot(band, jnp.where(same, 1.0, 0.0))
        kept = jnp.where(
            (iota(full, 1) >> log2(PS)) == (iota(full, 0) & 7), spread_lanes, 0.0
        )
        rows = exact_dot(slot_pick, jnp.sum(kept.reshape(count * 2, 8, LANES), axis=1))
        for d in range(ndev):
            slots[d] = rows[2 * d : 2 * d + 2, :]

        def send_lift(i, carry):
            d = (me + i) % ndev
            pltpu.make_async_remote_copy(
                src_ref=slots.at[d], dst_ref=lifts.at[blk],
                send_sem=lift_send, recv_sem=lift_recv,
                device_id=coords(d), device_id_type=MESH,
            ).start()
            return carry

        lax.fori_loop(1, ndev, send_lift, 0)
        lifts[blk] = slots[me]

    for k in range(4, 6):
        pl.when(halos[k][1])(halos[k][2].wait_recv)

    def layer(z, carry):
        for row0 in range(0, cx, 16):
            sixes = {}

            def six(f):
                if f not in sixes:
                    sixes[f] = six_neighbours(ext, yl, yr, f, z, z + 1, 16, row0, depth)
                return sixes[f]

            def across(f, along):
                return six(f)[2 * along] - six(f)[2 * along + 1]

            def put(f, rate):
                outv[f, z, row0 : row0 + 16, :] = mean_of(six(f)) + wave_ratio * rate

            buoyancy = mat[0, z, row0 : row0 + 16, :]
            lame = mat[1, z, row0 : row0 + 16, :]
            shear = mat[2, z, row0 : row0 + 16, :]
            dx, dy, dz = across(0, 1), across(1, 2), across(2, 0)
            ldiv = lame * (dx + dy + dz)
            put(0, buoyancy * (across(3, 1) + across(6, 2) + across(7, 0)))
            put(1, buoyancy * (across(6, 1) + across(4, 2) + across(8, 0)))
            put(2, buoyancy * (across(7, 1) + across(8, 2) + across(5, 0)))
            put(3, ldiv + 2.0 * shear * dx)
            put(4, ldiv + 2.0 * shear * dy)
            put(5, ldiv + 2.0 * shear * dz)
            put(6, shear * (across(0, 2) + across(1, 1)))
            put(7, shear * (across(0, 0) + across(2, 1)))
            put(8, shear * (across(1, 0) + across(2, 2)))
        return carry

    first_part = depth // 2
    lax.fori_loop(0, first_part, layer, 0)

    some = strips.at[gz, pl.ds(0, nblk - 1)]
    pltpu.make_async_copy(some, some, st_recv).wait()

    def hand(i):
        other = (gz + i) % ngz
        return pltpu.make_async_remote_copy(
            src_ref=strips.at[gz], dst_ref=strips.at[gz],
            send_sem=sib_send.at[i - 1], recv_sem=sib_recv.at[i - 1],
            device_id=(gx, gy, other), device_id_type=MESH,
        )

    for i in range(1, ngz):
        hand(i).start()
    lax.fori_loop(first_part, depth, layer, 0)

    for i in range(1, ngz):
        hand(i).wait_recv()
    ghosts_out[...] = exact_dot(pick_all, strips[...].reshape(ndev * 24, LANES))

    @pl.when(gz == 0)
    def _():
        part = lifts.at[pl.ds(0, nblk - 1)]
        pltpu.make_async_copy(part, part, lift_recv).wait()

    @pl.when(gz != 0)
    def _():
        pltpu.make_async_copy(lifts, lifts, lift_recv).wait()

    for k in range(2):
        coarse_out[k] = exact_dot(chooser, lifts[:, k, :])

    for has_target, _, copy in halos:
        pl.when(has_target)(copy.wait_send)
    pltpu.make_async_copy(some, some, st_send).wait()
    for i in range(1, ngz):
        hand(i).wait_send()

    @pl.when(gz == 0)
    def _():
        sent = slots.at[pl.ds(0, ndev - 1)]
        pltpu.make_async_copy(sent, sent, lift_send).wait()


def finish(
    outv, state_ref, ghosts_ref, found_ref, coarse_ref, vout_hbm, wout_ref, out_sem
):
    store = pltpu.make_async_copy(outv, vout_hbm, out_sem)
    store.start()
    state = [state_ref[0], state_ref[1], state_ref[2]]
    groups = FP * FP // LANES
    wide_lane = iota((LANES, 8 * LANES), 1)
    source = (wide_lane >> log2(LANES)) * PS + ((wide_lane & (FP - 1)) >> log2(REFINE))
    expand = jnp.where(iota((LANES, 8 * LANES), 0) == source, 1.0, 0.0)
    fine = [exact_dot(coarse_ref[k], expand)[:PATCH_DEV] for k in range(2)]
    lift = jnp.concatenate(
        [
            fine[(k // 2) // 8][:, LANES * ((k // 2) % 8) : LANES * ((k // 2) % 8 + 1)]
            for k in range(groups)
        ],
        axis=1,
    )

    lane = iota((PATCH_DEV, FP * FP), 1)
    col = lane & (FP - 1)

    def ghost(side, c):
        at = (side * 3 + c) * 8
        return ghosts_ref[at : at + PATCH_DEV, :]

    def beside(c, side):
        st = state[c]
        g = ghost(side, c)
        found = found_ref[side, :PATCH_DEV, :1] > 0.5
        if side == 0:
            wide = jnp.concatenate([pltpu.roll(g, FP, 1)] * groups, axis=1)
            edge, moved = lane < FP, pltpu.roll(st, FP, 1)
        elif side == 1:
            wide = jnp.concatenate([pltpu.roll(g, FP, 1)] * groups, axis=1)
            edge, moved = lane >= FP * FP - FP, pltpu.roll(st, FP * FP - FP, 1)
        elif side == 2:
            wide = jnp.concatenate([pltpu.roll(g, 96 - k, 1) for k in range(groups)], axis=1)
            edge, moved = col == 0, pltpu.roll(st, 1, 1)
        else:
            wide = jnp.concatenate([pltpu.roll(g, 63 - k, 1) for k in range(groups)], axis=1)
            edge, moved = col == FP - 1, pltpu.roll(st, FP * FP - 1, 1)
        return jnp.where(edge, jnp.where(found, wide, st), moved)

    sides = [[beside(c, side) for c in range(3)] for side in range(4)]

    def fluxes_x(part):
        height, flow_x, flow_y = part
        speed = flow_x / height
        return [flow_x, flow_x * speed + 0.5 * gravity * height * height, flow_y * speed]

    def fluxes_y(part):
        height, flow_x, flow_y = part
        speed = flow_y / height
        return [flow_y, flow_x * speed, flow_y * speed + 0.5 * gravity * height * height]

    fw, fe = fluxes_x(sides[0]), fluxes_x(sides[1])
    fs, fn = fluxes_y(sides[2]), fluxes_y(sides[3])
    for c in range(3):
        updated = 0.25 * (sides[1][c] + sides[0][c] + sides[3][c] + sides[2][c]) - flux_ratio * (
            (fe[c] - fw[c]) + (fn[c] - fs[c])
        )
        if c == 0:
            updated = updated + uplift_rate * lift
        wout_ref[c] = updated
    store.wait()


def per_device(volume, materials, water_height, water_flow, owner_of, patch_tile):
    ngx, ngy, ngz = (lax.axis_size(a) for a in ("gx", "gy", "gz"))
    ndev, nblk = ngx * ngy * ngz, ngx * ngy
    fields, depth, cx, cy = volume.shape
    patches = owner_of.shape[0]
    assert cy == LANES and fields * depth <= LANES
    f32 = jnp.float32
    dma = pltpu.SemaphoreType.DMA
    vmem = pl.BlockSpec(memory_space=pltpu.VMEM)
    hbm = pl.BlockSpec(memory_space=pltpu.HBM)
    whole = functools.partial(pltpu.with_memory_space_constraint, memory_space=pltpu.VMEM)
    middle = pl.pallas_call(
        functools.partial(kernel, (ngx, ngy, ngz, patches, depth, cx)),
        name="coupled_step",
        out_shape=(
            pltpu.VMEM(volume.shape, f32),
            pltpu.VMEM((3,) + water_height.shape, f32),
            pltpu.VMEM((96, LANES), f32),
            pltpu.VMEM((4, 8, LANES), f32),
            pltpu.VMEM((2, 8, LANES), f32),
        ),
        in_specs=[hbm] * 6,
        out_specs=(vmem,) * 5,
        scratch_shapes=[
            pltpu.VMEM((fields, depth + 2, cx + 16, LANES), f32),
            pltpu.VMEM(materials.shape, f32),
            pltpu.VMEM((cx, LANES), f32),
            pltpu.VMEM((cx, LANES), f32),
            pltpu.VMEM((cx, LANES), f32),
            pltpu.VMEM((cx, LANES), f32),
            pltpu.VMEM((ngz, nblk, 24, LANES), f32),
            pltpu.VMEM((ndev, 2, LANES), f32),
            pltpu.VMEM((nblk, 2, LANES), f32),
            pltpu.VMEM((1, patches), jnp.int32), pltpu.VMEM((1, patches), jnp.int32),
            dma, dma, dma((4,)), dma((6,)), dma((6,)), dma, dma,
            dma((max(ngz - 1, 1),)), dma((max(ngz - 1, 1),)), dma, dma,
        ],
        compiler_params=pltpu.CompilerParams(
            collective_id=0, has_side_effects=True, vmem_limit_bytes=40 * 1024 * 1024
        ),
    )(
        owner_of.reshape(1, patches), patch_tile.reshape(1, patches),
        water_height, water_flow, volume, materials,
    )
    middle = [whole(part) for part in middle]
    return pl.pallas_call(
        finish,
        name="finish_step",
        out_shape=(
            jax.ShapeDtypeStruct(volume.shape, f32),
            jax.ShapeDtypeStruct((3,) + water_height.shape, f32),
        ),
        in_specs=[vmem] * 5,
        out_specs=(hbm, vmem),
        scratch_shapes=[dma],
        compiler_params=pltpu.CompilerParams(vmem_limit_bytes=16 * 1024 * 1024),
    )(*middle)


def solution(mesh):
    return jax.shard_map(
        per_device,
        mesh=mesh,
        in_specs=(
            P(None, "gz", "gx", "gy"),
            P(None, "gz", "gx", "gy"),
            P(("gx", "gy", "gz"), None),
            P(None, ("gx", "gy", "gz"), None),
            P(),
            P(),
        ),
        out_specs=(P(None, "gz", "gx", "gy"), P(None, ("gx", "gy", "gz"), None)),
        check_vma=False,
    )
```

```python
import functools

import jax
import jax.numpy as jnp
from jax import lax
from jax.experimental import pallas as pl
from jax.experimental.pallas import tpu as pltpu
from jax.sharding import PartitionSpec as P

PATCH_DEV = 4
PS = 16
REFINE = 4
FP = 64
LANES = 128
MESH = pl.DeviceIdType.MESH

wave_ratio = 0.075
flux_ratio = 0.05
uplift_rate = 1.0
gravity = 1.0


def log2(n):
    assert n & (n - 1) == 0
    return n.bit_length() - 1


def iota(shape, dim):
    return lax.broadcasted_iota(jnp.int32, shape, dim)


def exact_dot(a, b):
    return jnp.dot(a, b, precision=lax.Precision.HIGHEST, preferred_element_type=jnp.float32)


def pick_sum(mask, values):
    picked = jnp.where(mask, values.astype(jnp.float32), 0.0)
    return jnp.sum(picked, axis=1, keepdims=True).astype(jnp.int32)


def six_neighbours(ext, yl, yr, f, z, z_index, rows, row0, depth):
    lane = iota((rows, LANES), 1)
    at = f * depth + z
    top = row0 + 8
    mid = ext[f, z_index, top : top + rows, :]
    left = jnp.where(
        lane == 0,
        pltpu.roll(yl[row0 : row0 + rows, :], (LANES - at) & (LANES - 1), 1),
        pltpu.roll(mid, 1, 1),
    )
    right = jnp.where(
        lane == LANES - 1,
        pltpu.roll(yr[row0 : row0 + rows, :], LANES - 1 - at, 1),
        pltpu.roll(mid, LANES - 1, 1),
    )
    return (
        ext[f, z_index + 1, top : top + rows, :],
        ext[f, z_index - 1, top : top + rows, :],
        ext[f, z_index, top + 1 : top + 1 + rows, :],
        ext[f, z_index, top - 1 : top - 1 + rows, :],
        right,
        left,
    )


def mean_of(six):
    return (six[0] + six[1] + six[2] + six[3] + six[4] + six[5]) * (1.0 / 6.0)


def kernel(
    sizes,
    own_hbm, til_hbm, h_hbm, fl_hbm, vol_hbm, mat_hbm,
    outv, state_out, ghosts_out, found_out, coarse_out,
    ext, mat, ys_lo, ys_hi, yl, yr, strips, slots, lifts,
    own_ref, til_ref, vol_sem, mat_sem, in_sem, halo_send, halo_recv, st_send, st_recv, sib_send, sib_recv,
    lift_send, lift_recv,
):
    ngx, ngy, ngz, patches, depth, cx = sizes
    ndev = ngx * ngy * ngz
    nblk = ngx * ngy
    gx, gy, gz = lax.axis_index("gx"), lax.axis_index("gy"), lax.axis_index("gz")
    blk = gx * ngy + gy
    me = blk * ngz + gz
    local_x, local_y = cx // PS, LANES // PS
    tiles_x, tiles_y = local_x * ngx, local_y * ngy

    def coords(d):
        return (d // (ngy * ngz), (d // ngz) % ngy, d % ngz)

    vol_copy = pltpu.make_async_copy(
        vol_hbm, ext.at[:, pl.ds(1, depth), pl.ds(8, cx), :], vol_sem
    )
    ins = [
        pltpu.make_async_copy(h_hbm, state_out.at[0], in_sem.at[0]),
        pltpu.make_async_copy(fl_hbm, state_out.at[pl.ds(1, 2)], in_sem.at[1]),
        pltpu.make_async_copy(own_hbm, own_ref, in_sem.at[2]),
        pltpu.make_async_copy(til_hbm, til_ref, in_sem.at[3]),
    ]
    for copy in ins:
        copy.start()
    vol_copy.start()
    mat_copy = pltpu.make_async_copy(mat_hbm, mat, mat_sem)
    mat_copy.start()

    barrier = pltpu.get_barrier_semaphore()

    def greet(i, carry):
        pl.semaphore_signal(
            barrier, inc=1, device_id=coords((me + i) % ndev), device_id_type=MESH
        )
        return carry

    lax.fori_loop(1, ndev, greet, 0)

    @pl.when(gz == 0)
    def _():
        ext[:, 0] = jnp.zeros_like(ext[:, 0])

    @pl.when(gz == ngz - 1)
    def _():
        ext[:, depth + 1] = jnp.zeros_like(ext[:, depth + 1])

    @pl.when(gx == 0)
    def _():
        ext[:, 1 : depth + 1, 7:8, :] = jnp.zeros((9, depth, 1, LANES), jnp.float32)

    @pl.when(gx == ngx - 1)
    def _():
        ext[:, 1 : depth + 1, cx + 8 : cx + 9, :] = jnp.zeros((9, depth, 1, LANES), jnp.float32)

    @pl.when(gy == 0)
    def _():
        yl[...] = jnp.zeros_like(yl)

    @pl.when(gy == ngy - 1)
    def _():
        yr[...] = jnp.zeros_like(yr)

    lane4 = iota((PATCH_DEV, LANES), 1)
    half = lane4 & (FP - 1)
    for copy in ins:
        copy.wait()
    state = [state_out[0], state_out[1], state_out[2]]
    groups = FP * FP // LANES
    for c in range(3):
        st = state[c]
        strips[gz, blk, 4 * c : 4 * c + 4, :] = jnp.where(
            lane4 < FP, st[:, :LANES], st[:, FP * FP - LANES :]
        )
        packed = jnp.zeros((PATCH_DEV, LANES), jnp.float32)
        for k in range(groups):
            part = st[:, LANES * k : LANES * (k + 1)]
            first = part if k == 0 else pltpu.roll(part, k, 1)
            packed = jnp.where(half == k, first, packed)
            packed = jnp.where(half == 32 + k, pltpu.roll(part, (k + 97) % LANES, 1), packed)
        strips[gz, blk, 12 + 4 * c : 16 + 4 * c, :] = packed

    vol_copy.wait()

    lane_c = iota((cx, LANES), 1)

    def pack(z, carry):
        lo, hi = carry
        for f in range(9):
            at = f * depth + z
            u = ext[f, z + 1, 8 : 8 + cx, :]
            lo = jnp.where(lane_c == at, pltpu.roll(u, at, 1), lo)
            hi = jnp.where(lane_c == at, pltpu.roll(u, at + 1, 1), hi)
        return lo, hi

    zero_face = jnp.zeros((cx, LANES), jnp.float32)
    lo, hi = lax.fori_loop(0, depth, pack, (zero_face, zero_face))
    ys_lo[...] = lo
    ys_hi[...] = hi

    pl.semaphore_wait(barrier, ndev - 1)

    def remote(src, dst, k, target):
        return pltpu.make_async_remote_copy(
            src_ref=src, dst_ref=dst, send_sem=halo_send.at[k], recv_sem=halo_recv.at[k],
            device_id=target, device_id_type=MESH,
        )

    inner = pl.ds(1, depth)
    halos = [
        (gy < ngy - 1, gy > 0, remote(ys_hi, yl, 0, (gx, gy + 1, gz))),
        (gy > 0, gy < ngy - 1, remote(ys_lo, yr, 1, (gx, gy - 1, gz))),
        (gx < ngx - 1, gx > 0, remote(
            ext.at[:, inner, pl.ds(cx + 7, 1), :], ext.at[:, inner, pl.ds(7, 1), :],
            2, (gx + 1, gy, gz))),
        (gx > 0, gx < ngx - 1, remote(
            ext.at[:, inner, pl.ds(8, 1), :], ext.at[:, inner, pl.ds(cx + 8, 1), :],
            3, (gx - 1, gy, gz))),
        (gz < ngz - 1, gz > 0, remote(
            ext.at[:, depth, pl.ds(8, cx), :], ext.at[:, 0, pl.ds(8, cx), :],
            4, (gx, gy, gz + 1))),
        (gz > 0, gz < ngz - 1, remote(
            ext.at[:, 1, pl.ds(8, cx), :], ext.at[:, depth + 1, pl.ds(8, cx), :],
            5, (gx, gy, gz - 1))),
    ]
    for has_target, _, copy in halos:
        pl.when(has_target)(copy.start)

    def spread(i, carry):
        b = (blk + i) % nblk
        pltpu.make_async_remote_copy(
            src_ref=strips.at[gz, blk], dst_ref=strips.at[gz, blk],
            send_sem=st_send, recv_sem=st_recv,
            device_id=(b // ngy, b % ngy, gz), device_id_type=MESH,
        ).start()
        return carry

    lax.fori_loop(1, nblk, spread, 0)

    owner = own_ref[...]
    tile = til_ref[...]
    square = (patches, patches)
    owner_wide = jnp.broadcast_to(owner, square)
    owner_col = pick_sum(iota(square, 0) == iota(square, 1), owner_wide)
    earlier = (owner_col == owner_wide) & (iota(square, 0) < iota(square, 1))
    rank = jnp.sum(jnp.where(earlier, 1.0, 0.0), axis=0, keepdims=True).astype(jnp.int32)
    row_of = owner * PATCH_DEV + rank
    tile_x = tile >> log2(tiles_y)
    tile_y = tile & (tiles_y - 1)
    wide8 = (8, patches)
    row_of8 = jnp.broadcast_to(row_of, wide8)
    tile8 = jnp.broadcast_to(tile, wide8)
    mine = row_of8 == me * PATCH_DEV + iota(wide8, 0)
    mine = mine & (iota(wide8, 0) < PATCH_DEV)
    my_tile = pick_sum(mine, tile8)
    my_x = my_tile >> log2(tiles_y)
    my_y = my_tile & (tiles_y - 1)
    my_blk = (my_x >> log2(local_x)) * ngy + (my_y >> log2(local_y))

    picks = []
    keys = (8, ndev * 24)
    for side, (valid, want) in enumerate(
        [
            (my_x > 0, my_tile - tiles_y),
            (my_x < tiles_x - 1, my_tile + tiles_y),
            (my_y > 0, my_tile - 1),
            (my_y < tiles_y - 1, my_tile + 1),
        ]
    ):
        match = tile8 == jnp.where(valid, want, -1)
        other = pick_sum(match, row_of8 + 1) - 1
        found_out[side] = jnp.broadcast_to(jnp.where(other >= 0, 1.0, 0.0), (8, LANES))
        dev = other >> log2(PATCH_DEV)
        place = (dev & (ngz - 1)) * nblk + (dev >> log2(ngz))
        target = place * 24 + (other & (PATCH_DEV - 1))
        for c in range(3):
            q = c if side < 2 else 3 + c
            goal = jnp.where(other >= 0, target + 4 * q, -1)
            picks.append(jnp.where(iota(keys, 1) == goal, 1.0, 0.0))
    pick_all = jnp.concatenate(picks, axis=0)

    chooser = jnp.where(iota((8, nblk), 1) == my_blk, 1.0, 0.0)
    here = (tile_x >> log2(local_x) == gx) & (tile_y >> log2(local_y) == gy)
    here_wide = jnp.broadcast_to(jnp.where(here, 1, 0), square)
    here_col = pick_sum(iota(square, 0) == iota(square, 1), here_wide)
    before = (here_col == 1) & (iota(square, 0) < iota(square, 1))
    place_row = jnp.sum(jnp.where(before, 1.0, 0.0), axis=0, keepdims=True).astype(jnp.int32)
    place_row = jnp.where(here, place_row, -1)
    count = PATCH_DEV * ngz
    tall = (count * PS, patches)
    chosen = jnp.broadcast_to(place_row, tall) == (iota(tall, 0) >> log2(PS))
    local = (tile_x & (local_x - 1)) * local_y + (tile_y & (local_y - 1)) + 1
    local_col = pick_sum(chosen, jnp.broadcast_to(local, tall)) - 1
    local_tx = local_col >> log2(local_y)
    local_ty = local_col & (local_y - 1)
    row_want = local_tx * PS + (iota((count * PS, 1), 0) & (PS - 1))
    row_pick = jnp.where(iota((count * PS, cx), 1) == row_want, 1.0, 0.0)
    full = (count * PS, LANES)
    lane_pick = (iota(full, 1) >> log2(PS)) == local_ty
    owner_here = jnp.where(here, owner, -1)
    slot_wide = (2 * ndev, patches)
    owned = jnp.broadcast_to(owner_here, slot_wide) == (iota(slot_wide, 0) >> 1)
    slot_place = pick_sum(owned, jnp.broadcast_to(place_row + 1, slot_wide)) - 1
    slot_row = jnp.where(slot_place >= 0, 2 * slot_place + (iota((2 * ndev, 1), 0) & 1), -1)
    slot_pick = jnp.where(iota((2 * ndev, 2 * count), 1) == slot_row, 1.0, 0.0)

    for k in range(4):
        pl.when(halos[k][1])(halos[k][2].wait_recv)
    mat_copy.wait()

    @pl.when(gz == 0)
    def _():
        def six(f):
            return six_neighbours(ext, yl, yr, f, 0, 1, cx, 0, depth)

        vz = six(2)
        sxz, syz = six(7), six(8)
        szz = ext[5, 2, 8 : 8 + cx, :] - ext[5, 0, 8 : 8 + cx, :]
        rate = mat[0, 0] * ((sxz[2] - sxz[3]) + (syz[4] - syz[5]) + szz)
        floor = mean_of(vz) + wave_ratio * rate
        band = jnp.where(lane_pick, exact_dot(row_pick, floor), 0.0)
        same = (iota((LANES, LANES), 0) & (PS - 1)) == (iota((LANES, LANES), 1) & (PS - 1))
        spread_lanes = exact_dot(band, jnp.where(same, 1.0, 0.0))
        kept = jnp.where(
            (iota(full, 1) >> log2(PS)) == (iota(full, 0) & 7), spread_lanes, 0.0
        )
        rows = exact_dot(slot_pick, jnp.sum(kept.reshape(count * 2, 8, LANES), axis=1))
        for d in range(ndev):
            slots[d] = rows[2 * d : 2 * d + 2, :]

        def send_lift(i, carry):
            d = (me + i) % ndev
            pltpu.make_async_remote_copy(
                src_ref=slots.at[d], dst_ref=lifts.at[blk],
                send_sem=lift_send, recv_sem=lift_recv,
                device_id=coords(d), device_id_type=MESH,
            ).start()
            return carry

        lax.fori_loop(1, ndev, send_lift, 0)
        lifts[blk] = slots[me]

    for k in range(4, 6):
        pl.when(halos[k][1])(halos[k][2].wait_recv)

    def layer(z, carry):
        for row0 in range(0, cx, 16):
            sixes = {}

            def six(f):
                if f not in sixes:
                    sixes[f] = six_neighbours(ext, yl, yr, f, z, z + 1, 16, row0, depth)
                return sixes[f]

            def across(f, along):
                return six(f)[2 * along] - six(f)[2 * along + 1]

            def put(f, rate):
                outv[f, z, row0 : row0 + 16, :] = mean_of(six(f)) + wave_ratio * rate

            buoyancy = mat[0, z, row0 : row0 + 16, :]
            lame = mat[1, z, row0 : row0 + 16, :]
            shear = mat[2, z, row0 : row0 + 16, :]
            dx, dy, dz = across(0, 1), across(1, 2), across(2, 0)
            ldiv = lame * (dx + dy + dz)
            put(0, buoyancy * (across(3, 1) + across(6, 2) + across(7, 0)))
            put(1, buoyancy * (across(6, 1) + across(4, 2) + across(8, 0)))
            put(2, buoyancy * (across(7, 1) + across(8, 2) + across(5, 0)))
            put(3, ldiv + 2.0 * shear * dx)
            put(4, ldiv + 2.0 * shear * dy)
            put(5, ldiv + 2.0 * shear * dz)
            put(6, shear * (across(0, 2) + across(1, 1)))
            put(7, shear * (across(0, 0) + across(2, 1)))
            put(8, shear * (across(1, 0) + across(2, 2)))
        return carry

    first_part = depth // 2
    lax.fori_loop(0, first_part, layer, 0)

    some = strips.at[gz, pl.ds(0, nblk - 1)]
    pltpu.make_async_copy(some, some, st_recv).wait()

    def hand(i):
        other = (gz + i) % ngz
        return pltpu.make_async_remote_copy(
            src_ref=strips.at[gz], dst_ref=strips.at[gz],
            send_sem=sib_send.at[i - 1], recv_sem=sib_recv.at[i - 1],
            device_id=(gx, gy, other), device_id_type=MESH,
        )

    for i in range(1, ngz):
        hand(i).start()
    lax.fori_loop(first_part, depth, layer, 0)

    for i in range(1, ngz):
        hand(i).wait_recv()
    ghosts_out[...] = exact_dot(pick_all, strips[...].reshape(ndev * 24, LANES))

    @pl.when(gz == 0)
    def _():
        part = lifts.at[pl.ds(0, nblk - 1)]
        pltpu.make_async_copy(part, part, lift_recv).wait()

    @pl.when(gz != 0)
    def _():
        pltpu.make_async_copy(lifts, lifts, lift_recv).wait()

    for k in range(2):
        coarse_out[k] = exact_dot(chooser, lifts[:, k, :])

    for has_target, _, copy in halos:
        pl.when(has_target)(copy.wait_send)
    pltpu.make_async_copy(some, some, st_send).wait()
    for i in range(1, ngz):
        hand(i).wait_send()

    @pl.when(gz == 0)
    def _():
        sent = slots.at[pl.ds(0, ndev - 1)]
        pltpu.make_async_copy(sent, sent, lift_send).wait()


def finish(
    outv, state_ref, ghosts_ref, found_ref, coarse_ref, vout_hbm, wout_ref, out_sem
):
    store = pltpu.make_async_copy(outv, vout_hbm, out_sem)
    store.start()
    state = [state_ref[0], state_ref[1], state_ref[2]]
    groups = FP * FP // LANES
    wide_lane = iota((LANES, 8 * LANES), 1)
    source = (wide_lane >> log2(LANES)) * PS + ((wide_lane & (FP - 1)) >> log2(REFINE))
    expand = jnp.where(iota((LANES, 8 * LANES), 0) == source, 1.0, 0.0)
    fine = [exact_dot(coarse_ref[k], expand)[:PATCH_DEV] for k in range(2)]
    lift = jnp.concatenate(
        [
            fine[(k // 2) // 8][:, LANES * ((k // 2) % 8) : LANES * ((k // 2) % 8 + 1)]
            for k in range(groups)
        ],
        axis=1,
    )

    lane = iota((PATCH_DEV, FP * FP), 1)
    col = lane & (FP - 1)

    def ghost(side, c):
        at = (side * 3 + c) * 8
        return ghosts_ref[at : at + PATCH_DEV, :]

    def beside(c, side):
        st = state[c]
        g = ghost(side, c)
        found = found_ref[side, :PATCH_DEV, :1] > 0.5
        if side == 0:
            wide = jnp.concatenate([pltpu.roll(g, FP, 1)] * groups, axis=1)
            edge, moved = lane < FP, pltpu.roll(st, FP, 1)
        elif side == 1:
            wide = jnp.concatenate([pltpu.roll(g, FP, 1)] * groups, axis=1)
            edge, moved = lane >= FP * FP - FP, pltpu.roll(st, FP * FP - FP, 1)
        elif side == 2:
            wide = jnp.concatenate([pltpu.roll(g, 96 - k, 1) for k in range(groups)], axis=1)
            edge, moved = col == 0, pltpu.roll(st, 1, 1)
        else:
            wide = jnp.concatenate([pltpu.roll(g, 63 - k, 1) for k in range(groups)], axis=1)
            edge, moved = col == FP - 1, pltpu.roll(st, FP * FP - 1, 1)
        return jnp.where(edge, jnp.where(found, wide, st), moved)

    sides = [[beside(c, side) for c in range(3)] for side in range(4)]

    def fluxes_x(part):
        height, flow_x, flow_y = part
        speed = flow_x / height
        return [flow_x, flow_x * speed + 0.5 * gravity * height * height, flow_y * speed]

    def fluxes_y(part):
        height, flow_x, flow_y = part
        speed = flow_y / height
        return [flow_y, flow_x * speed, flow_y * speed + 0.5 * gravity * height * height]

    fw, fe = fluxes_x(sides[0]), fluxes_x(sides[1])
    fs, fn = fluxes_y(sides[2]), fluxes_y(sides[3])
    for c in range(3):
        updated = 0.25 * (sides[1][c] + sides[0][c] + sides[3][c] + sides[2][c]) - flux_ratio * (
            (fe[c] - fw[c]) + (fn[c] - fs[c])
        )
        if c == 0:
            updated = updated + uplift_rate * lift
        wout_ref[c] = updated
    store.wait()


def per_device(volume, materials, water_height, water_flow, owner_of, patch_tile):
    ngx, ngy, ngz = (lax.axis_size(a) for a in ("gx", "gy", "gz"))
    ndev, nblk = ngx * ngy * ngz, ngx * ngy
    fields, depth, cx, cy = volume.shape
    patches = owner_of.shape[0]
    assert cy == LANES and fields * depth <= LANES
    f32 = jnp.float32
    dma = pltpu.SemaphoreType.DMA
    vmem = pl.BlockSpec(memory_space=pltpu.VMEM)
    hbm = pl.BlockSpec(memory_space=pltpu.HBM)
    whole = functools.partial(pltpu.with_memory_space_constraint, memory_space=pltpu.VMEM)
    middle = pl.pallas_call(
        functools.partial(kernel, (ngx, ngy, ngz, patches, depth, cx)),
        name="coupled_step",
        out_shape=(
            pltpu.VMEM(volume.shape, f32),
            pltpu.VMEM((3,) + water_height.shape, f32),
            pltpu.VMEM((96, LANES), f32),
            pltpu.VMEM((4, 8, LANES), f32),
            pltpu.VMEM((2, 8, LANES), f32),
        ),
        in_specs=[hbm] * 6,
        out_specs=(vmem,) * 5,
        scratch_shapes=[
            pltpu.VMEM((fields, depth + 2, cx + 16, LANES), f32),
            pltpu.VMEM(materials.shape, f32),
            pltpu.VMEM((cx, LANES), f32),
            pltpu.VMEM((cx, LANES), f32),
            pltpu.VMEM((cx, LANES), f32),
            pltpu.VMEM((cx, LANES), f32),
            pltpu.VMEM((ngz, nblk, 24, LANES), f32),
            pltpu.VMEM((ndev, 2, LANES), f32),
            pltpu.VMEM((nblk, 2, LANES), f32),
            pltpu.VMEM((1, patches), jnp.int32), pltpu.VMEM((1, patches), jnp.int32),
            dma, dma, dma((4,)), dma((6,)), dma((6,)), dma, dma,
            dma((max(ngz - 1, 1),)), dma((max(ngz - 1, 1),)), dma, dma,
        ],
        compiler_params=pltpu.CompilerParams(
            collective_id=0, has_side_effects=True, vmem_limit_bytes=40 * 1024 * 1024
        ),
    )(
        *[
            pltpu.with_memory_space_constraint(part, pltpu.HBM)
            for part in (
                owner_of.reshape(1, patches), patch_tile.reshape(1, patches),
                water_height, water_flow, volume, materials,
            )
        ]
    )
    middle = [whole(part) for part in middle]
    return pl.pallas_call(
        finish,
        name="finish_step",
        out_shape=(
            jax.ShapeDtypeStruct(volume.shape, f32),
            jax.ShapeDtypeStruct((3,) + water_height.shape, f32),
        ),
        in_specs=[vmem] * 5,
        out_specs=(hbm, vmem),
        scratch_shapes=[dma],
        compiler_params=pltpu.CompilerParams(vmem_limit_bytes=16 * 1024 * 1024),
    )(*middle)


def solution(mesh):
    return jax.shard_map(
        per_device,
        mesh=mesh,
        in_specs=(
            P(None, "gz", "gx", "gy"),
            P(None, "gz", "gx", "gy"),
            P(("gx", "gy", "gz"), None),
            P(None, ("gx", "gy", "gz"), None),
            P(),
            P(),
        ),
        out_specs=(P(None, "gz", "gx", "gy"), P(None, ("gx", "gy", "gz"), None)),
        check_vma=False,
    )
```

```python
import functools

import jax
import jax.numpy as jnp
from jax import lax
from jax.experimental import pallas as pl
from jax.experimental.pallas import tpu as pltpu
from jax.sharding import PartitionSpec as P

PATCH_DEV = 4
PS = 16
REFINE = 4
FP = 64
LANES = 128
MESH = pl.DeviceIdType.MESH

wave_ratio = 0.075
flux_ratio = 0.05
uplift_rate = 1.0
gravity = 1.0


def log2(n):
    assert n & (n - 1) == 0
    return n.bit_length() - 1


def iota(shape, dim):
    return lax.broadcasted_iota(jnp.int32, shape, dim)


def exact_dot(a, b):
    return jnp.dot(a, b, precision=lax.Precision.HIGHEST, preferred_element_type=jnp.float32)


def pick_sum(mask, values):
    picked = jnp.where(mask, values.astype(jnp.float32), 0.0)
    return jnp.sum(picked, axis=1, keepdims=True).astype(jnp.int32)


def six_neighbours(ext, yl, yr, f, z, z_index, rows, row0, depth):
    lane = iota((rows, LANES), 1)
    at = f * depth + z
    top = row0 + 8
    mid = ext[f, z_index, top : top + rows, :]
    left = jnp.where(
        lane == 0,
        pltpu.roll(yl[row0 : row0 + rows, :], (LANES - at) & (LANES - 1), 1),
        pltpu.roll(mid, 1, 1),
    )
    right = jnp.where(
        lane == LANES - 1,
        pltpu.roll(yr[row0 : row0 + rows, :], LANES - 1 - at, 1),
        pltpu.roll(mid, LANES - 1, 1),
    )
    return (
        ext[f, z_index + 1, top : top + rows, :],
        ext[f, z_index - 1, top : top + rows, :],
        ext[f, z_index, top + 1 : top + 1 + rows, :],
        ext[f, z_index, top - 1 : top - 1 + rows, :],
        right,
        left,
    )


def mean_of(six):
    return (six[0] + six[1] + six[2] + six[3] + six[4] + six[5]) * (1.0 / 6.0)


def neighbour_terms(part):
    height, flow_x, flow_y = part
    speed_x, speed_y = flow_x / height, flow_y / height
    head = 0.5 * gravity * height * height
    flux_x = [flow_x, flow_x * speed_x + head, flow_y * speed_x]
    flux_y = [flow_y, flow_x * speed_y, flow_y * speed_y + head]
    return [
        [0.25 * u + sign * flux_ratio * f for u, f in zip(part, flux)]
        for flux in (flux_x, flux_y)
        for sign in (1.0, -1.0)
    ]


def kernel(
    sizes,
    own_hbm, til_hbm, h_hbm, fl_hbm, vol_hbm, mat_hbm,
    outv, base_out, delta_out, coarse_out,
    state_in, ext, mat, ys_lo, ys_hi, yl, yr, strips, slots, lifts,
    own_ref, til_ref, vol_sem, mat_sem, in_sem, halo_send, halo_recv, st_send, st_recv, sib_send, sib_recv,
    lift_send, lift_recv,
):
    ngx, ngy, ngz, patches, depth, cx = sizes
    ndev = ngx * ngy * ngz
    nblk = ngx * ngy
    gx, gy, gz = lax.axis_index("gx"), lax.axis_index("gy"), lax.axis_index("gz")
    blk = gx * ngy + gy
    me = blk * ngz + gz
    local_x, local_y = cx // PS, LANES // PS
    tiles_x, tiles_y = local_x * ngx, local_y * ngy

    def coords(d):
        return (d // (ngy * ngz), (d // ngz) % ngy, d % ngz)

    vol_copy = pltpu.make_async_copy(
        vol_hbm, ext.at[:, pl.ds(1, depth), pl.ds(8, cx), :], vol_sem
    )
    ins = [
        pltpu.make_async_copy(h_hbm, state_in.at[0], in_sem.at[0]),
        pltpu.make_async_copy(fl_hbm, state_in.at[pl.ds(1, 2)], in_sem.at[1]),
        pltpu.make_async_copy(own_hbm, own_ref, in_sem.at[2]),
        pltpu.make_async_copy(til_hbm, til_ref, in_sem.at[3]),
    ]
    for copy in ins:
        copy.start()
    vol_copy.start()
    mat_copy = pltpu.make_async_copy(mat_hbm, mat, mat_sem)
    mat_copy.start()

    barrier = pltpu.get_barrier_semaphore()

    def greet(i, carry):
        pl.semaphore_signal(
            barrier, inc=1, device_id=coords((me + i) % ndev), device_id_type=MESH
        )
        return carry

    lax.fori_loop(1, ndev, greet, 0)

    @pl.when(gz == 0)
    def _():
        ext[:, 0] = jnp.zeros_like(ext[:, 0])

    @pl.when(gz == ngz - 1)
    def _():
        ext[:, depth + 1] = jnp.zeros_like(ext[:, depth + 1])

    @pl.when(gx == 0)
    def _():
        ext[:, 1 : depth + 1, 7:8, :] = jnp.zeros((9, depth, 1, LANES), jnp.float32)

    @pl.when(gx == ngx - 1)
    def _():
        ext[:, 1 : depth + 1, cx + 8 : cx + 9, :] = jnp.zeros((9, depth, 1, LANES), jnp.float32)

    @pl.when(gy == 0)
    def _():
        yl[...] = jnp.zeros_like(yl)

    @pl.when(gy == ngy - 1)
    def _():
        yr[...] = jnp.zeros_like(yr)

    lane4 = iota((PATCH_DEV, LANES), 1)
    half = lane4 & (FP - 1)
    for copy in ins:
        copy.wait()
    state = [state_in[0], state_in[1], state_in[2]]
    groups = FP * FP // LANES
    rows_own, cols_own = [], []
    for c in range(3):
        st = state[c]
        rows_own.append(jnp.where(lane4 < FP, st[:, :LANES], st[:, FP * FP - LANES :]))
        strips[gz, blk, 4 * c : 4 * c + 4, :] = rows_own[c]
        packed = jnp.zeros((PATCH_DEV, LANES), jnp.float32)
        for k in range(groups):
            part = st[:, LANES * k : LANES * (k + 1)]
            first = part if k == 0 else pltpu.roll(part, k, 1)
            packed = jnp.where(half == k, first, packed)
            packed = jnp.where(half == 32 + k, pltpu.roll(part, (k + 97) % LANES, 1), packed)
        cols_own.append(packed)
        strips[gz, blk, 12 + 4 * c : 16 + 4 * c, :] = packed

    lane_w = iota((PATCH_DEV, FP * FP), 1)
    col_w = lane_w & (FP - 1)
    span = FP * FP
    terms = neighbour_terms(state)
    moves = [
        (lane_w < FP, FP),
        (lane_w >= span - FP, span - FP),
        (col_w == 0, 1),
        (col_w == FP - 1, span - 1),
    ]
    for c in range(3):
        moved = [
            jnp.where(edge, terms[side][c], pltpu.roll(terms[side][c], shift, 1))
            for side, (edge, shift) in enumerate(moves)
        ]
        base_out[c] = (moved[0] + moved[1]) + (moved[2] + moved[3])

    vol_copy.wait()

    lane_c = iota((cx, LANES), 1)

    def pack(z, carry):
        lo, hi = carry
        for f in range(9):
            at = f * depth + z
            u = ext[f, z + 1, 8 : 8 + cx, :]
            lo = jnp.where(lane_c == at, pltpu.roll(u, at, 1), lo)
            hi = jnp.where(lane_c == at, pltpu.roll(u, at + 1, 1), hi)
        return lo, hi

    zero_face = jnp.zeros((cx, LANES), jnp.float32)
    lo, hi = lax.fori_loop(0, depth, pack, (zero_face, zero_face))
    ys_lo[...] = lo
    ys_hi[...] = hi

    pl.semaphore_wait(barrier, ndev - 1)

    def remote(src, dst, k, target):
        return pltpu.make_async_remote_copy(
            src_ref=src, dst_ref=dst, send_sem=halo_send.at[k], recv_sem=halo_recv.at[k],
            device_id=target, device_id_type=MESH,
        )

    inner = pl.ds(1, depth)
    halos = [
        (gy < ngy - 1, gy > 0, remote(ys_hi, yl, 0, (gx, gy + 1, gz))),
        (gy > 0, gy < ngy - 1, remote(ys_lo, yr, 1, (gx, gy - 1, gz))),
        (gx < ngx - 1, gx > 0, remote(
            ext.at[:, inner, pl.ds(cx + 7, 1), :], ext.at[:, inner, pl.ds(7, 1), :],
            2, (gx + 1, gy, gz))),
        (gx > 0, gx < ngx - 1, remote(
            ext.at[:, inner, pl.ds(8, 1), :], ext.at[:, inner, pl.ds(cx + 8, 1), :],
            3, (gx - 1, gy, gz))),
        (gz < ngz - 1, gz > 0, remote(
            ext.at[:, depth, pl.ds(8, cx), :], ext.at[:, 0, pl.ds(8, cx), :],
            4, (gx, gy, gz + 1))),
        (gz > 0, gz < ngz - 1, remote(
            ext.at[:, 1, pl.ds(8, cx), :], ext.at[:, depth + 1, pl.ds(8, cx), :],
            5, (gx, gy, gz - 1))),
    ]
    for has_target, _, copy in halos:
        pl.when(has_target)(copy.start)

    def spread(i, carry):
        b = (blk + i) % nblk
        pltpu.make_async_remote_copy(
            src_ref=strips.at[gz, blk], dst_ref=strips.at[gz, blk],
            send_sem=st_send, recv_sem=st_recv,
            device_id=(b // ngy, b % ngy, gz), device_id_type=MESH,
        ).start()
        return carry

    lax.fori_loop(1, nblk, spread, 0)

    owner = own_ref[...]
    tile = til_ref[...]
    square = (patches, patches)
    owner_wide = jnp.broadcast_to(owner, square)
    owner_col = pick_sum(iota(square, 0) == iota(square, 1), owner_wide)
    earlier = (owner_col == owner_wide) & (iota(square, 0) < iota(square, 1))
    rank = jnp.sum(jnp.where(earlier, 1.0, 0.0), axis=0, keepdims=True).astype(jnp.int32)
    row_of = owner * PATCH_DEV + rank
    tile_x = tile >> log2(tiles_y)
    tile_y = tile & (tiles_y - 1)
    wide8 = (8, patches)
    row_of8 = jnp.broadcast_to(row_of, wide8)
    tile8 = jnp.broadcast_to(tile, wide8)
    mine = row_of8 == me * PATCH_DEV + iota(wide8, 0)
    mine = mine & (iota(wide8, 0) < PATCH_DEV)
    my_tile = pick_sum(mine, tile8)
    my_x = my_tile >> log2(tiles_y)
    my_y = my_tile & (tiles_y - 1)
    my_blk = (my_x >> log2(local_x)) * ngy + (my_y >> log2(local_y))

    founds, picks = [], []
    keys = (8, ndev * 24)
    for side, (valid, want) in enumerate(
        [
            (my_x > 0, my_tile - tiles_y),
            (my_x < tiles_x - 1, my_tile + tiles_y),
            (my_y > 0, my_tile - 1),
            (my_y < tiles_y - 1, my_tile + 1),
        ]
    ):
        match = tile8 == jnp.where(valid, want, -1)
        other = pick_sum(match, row_of8 + 1) - 1
        founds.append((other >= 0)[:PATCH_DEV])
        dev = other >> log2(PATCH_DEV)
        place = (dev & (ngz - 1)) * nblk + (dev >> log2(ngz))
        target = place * 24 + (other & (PATCH_DEV - 1))
        for c in range(3):
            q = c if side < 2 else 3 + c
            goal = jnp.where(other >= 0, target + 4 * q, -1)
            picks.append(jnp.where(iota(keys, 1) == goal, 1.0, 0.0))
    pick_all = jnp.concatenate(picks, axis=0)

    chooser = jnp.where(iota((8, nblk), 1) == my_blk, 1.0, 0.0)
    here = (tile_x >> log2(local_x) == gx) & (tile_y >> log2(local_y) == gy)
    here_wide = jnp.broadcast_to(jnp.where(here, 1, 0), square)
    here_col = pick_sum(iota(square, 0) == iota(square, 1), here_wide)
    before = (here_col == 1) & (iota(square, 0) < iota(square, 1))
    place_row = jnp.sum(jnp.where(before, 1.0, 0.0), axis=0, keepdims=True).astype(jnp.int32)
    place_row = jnp.where(here, place_row, -1)
    count = PATCH_DEV * ngz
    tall = (count * PS, patches)
    chosen = jnp.broadcast_to(place_row, tall) == (iota(tall, 0) >> log2(PS))
    local = (tile_x & (local_x - 1)) * local_y + (tile_y & (local_y - 1)) + 1
    local_col = pick_sum(chosen, jnp.broadcast_to(local, tall)) - 1
    local_tx = local_col >> log2(local_y)
    local_ty = local_col & (local_y - 1)
    row_want = local_tx * PS + (iota((count * PS, 1), 0) & (PS - 1))
    row_pick = jnp.where(iota((count * PS, cx), 1) == row_want, 1.0, 0.0)
    full = (count * PS, LANES)
    lane_pick = (iota(full, 1) >> log2(PS)) == local_ty
    owner_here = jnp.where(here, owner, -1)
    slot_wide = (2 * ndev, patches)
    owned = jnp.broadcast_to(owner_here, slot_wide) == (iota(slot_wide, 0) >> 1)
    slot_place = pick_sum(owned, jnp.broadcast_to(place_row + 1, slot_wide)) - 1
    slot_row = jnp.where(slot_place >= 0, 2 * slot_place + (iota((2 * ndev, 1), 0) & 1), -1)
    slot_pick = jnp.where(iota((2 * ndev, 2 * count), 1) == slot_row, 1.0, 0.0)

    for k in range(4):
        pl.when(halos[k][1])(halos[k][2].wait_recv)
    mat_copy.wait()

    @pl.when(gz == 0)
    def _():
        def six(f):
            return six_neighbours(ext, yl, yr, f, 0, 1, cx, 0, depth)

        vz = six(2)
        sxz, syz = six(7), six(8)
        szz = ext[5, 2, 8 : 8 + cx, :] - ext[5, 0, 8 : 8 + cx, :]
        rate = mat[0, 0] * ((sxz[2] - sxz[3]) + (syz[4] - syz[5]) + szz)
        floor = mean_of(vz) + wave_ratio * rate
        band = jnp.where(lane_pick, exact_dot(row_pick, floor), 0.0)
        same = (iota((LANES, LANES), 0) & (PS - 1)) == (iota((LANES, LANES), 1) & (PS - 1))
        spread_lanes = exact_dot(band, jnp.where(same, 1.0, 0.0))
        kept = jnp.where(
            (iota(full, 1) >> log2(PS)) == (iota(full, 0) & 7), spread_lanes, 0.0
        )
        rows = exact_dot(slot_pick, jnp.sum(kept.reshape(count * 2, 8, LANES), axis=1))
        for d in range(ndev):
            slots[d] = rows[2 * d : 2 * d + 2, :]

        def send_lift(i, carry):
            d = (me + i) % ndev
            pltpu.make_async_remote_copy(
                src_ref=slots.at[d], dst_ref=lifts.at[blk],
                send_sem=lift_send, recv_sem=lift_recv,
                device_id=coords(d), device_id_type=MESH,
            ).start()
            return carry

        lax.fori_loop(1, ndev, send_lift, 0)
        lifts[blk] = slots[me]

    for k in range(4, 6):
        pl.when(halos[k][1])(halos[k][2].wait_recv)

    def layer(z, carry):
        for row0 in range(0, cx, 16):
            sixes = {}

            def six(f):
                if f not in sixes:
                    sixes[f] = six_neighbours(ext, yl, yr, f, z, z + 1, 16, row0, depth)
                return sixes[f]

            def across(f, along):
                return six(f)[2 * along] - six(f)[2 * along + 1]

            def put(f, rate):
                outv[f, z, row0 : row0 + 16, :] = mean_of(six(f)) + wave_ratio * rate

            buoyancy = mat[0, z, row0 : row0 + 16, :]
            lame = mat[1, z, row0 : row0 + 16, :]
            shear = mat[2, z, row0 : row0 + 16, :]
            dx, dy, dz = across(0, 1), across(1, 2), across(2, 0)
            ldiv = lame * (dx + dy + dz)
            put(0, buoyancy * (across(3, 1) + across(6, 2) + across(7, 0)))
            put(1, buoyancy * (across(6, 1) + across(4, 2) + across(8, 0)))
            put(2, buoyancy * (across(7, 1) + across(8, 2) + across(5, 0)))
            put(3, ldiv + 2.0 * shear * dx)
            put(4, ldiv + 2.0 * shear * dy)
            put(5, ldiv + 2.0 * shear * dz)
            put(6, shear * (across(0, 2) + across(1, 1)))
            put(7, shear * (across(0, 0) + across(2, 1)))
            put(8, shear * (across(1, 0) + across(2, 2)))
        return carry

    first_part = depth // 2
    lax.fori_loop(0, first_part, layer, 0)

    some = strips.at[gz, pl.ds(0, nblk - 1)]
    pltpu.make_async_copy(some, some, st_recv).wait()

    def hand(i):
        other = (gz + i) % ngz
        return pltpu.make_async_remote_copy(
            src_ref=strips.at[gz], dst_ref=strips.at[gz],
            send_sem=sib_send.at[i - 1], recv_sem=sib_recv.at[i - 1],
            device_id=(gx, gy, other), device_id_type=MESH,
        )

    for i in range(1, ngz):
        hand(i).start()
    lax.fori_loop(first_part, depth, layer, 0)

    for i in range(1, ngz):
        hand(i).wait_recv()
    ghosts = exact_dot(pick_all, strips[...].reshape(ndev * 24, LANES))

    changes = []
    for side, (own, shift) in enumerate(
        [(rows_own, FP), (rows_own, FP), (cols_own, 96), (cols_own, 32)]
    ):
        part = [
            jnp.where(
                founds[side],
                pltpu.roll(ghosts[at : at + PATCH_DEV, :], shift, 1),
                own[c],
            )
            for c, at in enumerate(range(side * 24, side * 24 + 24, 8))
        ]
        new, old = neighbour_terms(part)[side], neighbour_terms(own)[side]
        changes.append([new[c] - old[c] for c in range(3)])
    for c in range(3):
        delta_out[c, :PATCH_DEV, :] = jnp.where(lane4 < FP, changes[0][c], changes[1][c])
        delta_out[3 + c, :PATCH_DEV, :] = jnp.where(half < 32, changes[2][c], changes[3][c])

    @pl.when(gz == 0)
    def _():
        part = lifts.at[pl.ds(0, nblk - 1)]
        pltpu.make_async_copy(part, part, lift_recv).wait()

    @pl.when(gz != 0)
    def _():
        pltpu.make_async_copy(lifts, lifts, lift_recv).wait()

    for k in range(2):
        coarse_out[8 * k : 8 * k + 8, :] = exact_dot(chooser, lifts[:, k, :])

    for has_target, _, copy in halos:
        pl.when(has_target)(copy.wait_send)
    pltpu.make_async_copy(some, some, st_send).wait()
    for i in range(1, ngz):
        hand(i).wait_send()

    @pl.when(gz == 0)
    def _():
        sent = slots.at[pl.ds(0, ndev - 1)]
        pltpu.make_async_copy(sent, sent, lift_send).wait()


def finish(outv, base_ref, delta_ref, coarse_ref, vout_hbm, wout_ref, out_sem):
    store = pltpu.make_async_copy(outv, vout_hbm, out_sem)
    store.start()
    groups = FP * FP // LANES
    wide_lane = iota((LANES, 8 * LANES), 1)
    source = (wide_lane >> log2(LANES)) * PS + ((wide_lane & (FP - 1)) >> log2(REFINE))
    expand = jnp.where(iota((LANES, 8 * LANES), 0) == source, 1.0, 0.0)
    fine = exact_dot(coarse_ref[...], expand)
    lane4 = iota((PATCH_DEV, LANES), 1)
    half = lane4 & (FP - 1)
    for c in range(3):
        rows = delta_ref[c, :PATCH_DEV, :]
        cols = delta_ref[3 + c, :PATCH_DEV, :]
        for k in range(groups):
            at = pl.ds(LANES * k, LANES)
            value = base_ref[c, :, at]
            low = cols if k == 0 else pltpu.roll(cols, LANES - k, 1)
            high = cols if k == 31 else pltpu.roll(cols, (31 - k) % LANES, 1)
            value = value + jnp.where(half == 0, low, jnp.where(half == FP - 1, high, 0.0))
            if k == 0:
                value = value + jnp.where(lane4 < FP, rows, 0.0)
            if k == groups - 1:
                value = value + jnp.where(lane4 < FP, 0.0, rows)
            if c == 0:
                r = k // 2
                top = 8 * (r // 8)
                lift = fine[top : top + PATCH_DEV, LANES * (r % 8) : LANES * (r % 8 + 1)]
                value = value + uplift_rate * lift
            wout_ref[c, :, at] = value
    store.wait()


def per_device(volume, materials, water_height, water_flow, owner_of, patch_tile):
    ngx, ngy, ngz = (lax.axis_size(a) for a in ("gx", "gy", "gz"))
    ndev, nblk = ngx * ngy * ngz, ngx * ngy
    fields, depth, cx, cy = volume.shape
    patches = owner_of.shape[0]
    assert cy == LANES and fields * depth <= LANES
    f32 = jnp.float32
    dma = pltpu.SemaphoreType.DMA
    vmem = pl.BlockSpec(memory_space=pltpu.VMEM)
    hbm = pl.BlockSpec(memory_space=pltpu.HBM)
    whole = functools.partial(pltpu.with_memory_space_constraint, memory_space=pltpu.VMEM)
    middle = pl.pallas_call(
        functools.partial(kernel, (ngx, ngy, ngz, patches, depth, cx)),
        name="coupled_step",
        out_shape=(
            pltpu.VMEM(volume.shape, f32),
            pltpu.VMEM((3,) + water_height.shape, f32),
            pltpu.VMEM((6, 8, LANES), f32),
            pltpu.VMEM((16, LANES), f32),
        ),
        in_specs=[hbm] * 6,
        out_specs=(vmem,) * 4,
        scratch_shapes=[
            pltpu.VMEM((3,) + water_height.shape, f32),
            pltpu.VMEM((fields, depth + 2, cx + 16, LANES), f32),
            pltpu.VMEM(materials.shape, f32),
            pltpu.VMEM((cx, LANES), f32),
            pltpu.VMEM((cx, LANES), f32),
            pltpu.VMEM((cx, LANES), f32),
            pltpu.VMEM((cx, LANES), f32),
            pltpu.VMEM((ngz, nblk, 24, LANES), f32),
            pltpu.VMEM((ndev, 2, LANES), f32),
            pltpu.VMEM((nblk, 2, LANES), f32),
            pltpu.VMEM((1, patches), jnp.int32), pltpu.VMEM((1, patches), jnp.int32),
            dma, dma, dma((4,)), dma((6,)), dma((6,)), dma, dma,
            dma((max(ngz - 1, 1),)), dma((max(ngz - 1, 1),)), dma, dma,
        ],
        compiler_params=pltpu.CompilerParams(
            collective_id=0, has_side_effects=True, vmem_limit_bytes=40 * 1024 * 1024
        ),
    )(
        *[
            pltpu.with_memory_space_constraint(part, pltpu.HBM)
            for part in (
                owner_of.reshape(1, patches), patch_tile.reshape(1, patches),
                water_height, water_flow, volume, materials,
            )
        ]
    )
    middle = [whole(part) for part in middle]
    return pl.pallas_call(
        finish,
        name="finish_step",
        out_shape=(
            jax.ShapeDtypeStruct(volume.shape, f32),
            jax.ShapeDtypeStruct((3,) + water_height.shape, f32),
        ),
        in_specs=[vmem] * 4,
        out_specs=(hbm, vmem),
        scratch_shapes=[dma],
        compiler_params=pltpu.CompilerParams(vmem_limit_bytes=16 * 1024 * 1024),
    )(*middle)


def solution(mesh):
    return jax.shard_map(
        per_device,
        mesh=mesh,
        in_specs=(
            P(None, "gz", "gx", "gy"),
            P(None, "gz", "gx", "gy"),
            P(("gx", "gy", "gz"), None),
            P(None, ("gx", "gy", "gz"), None),
            P(),
            P(),
        ),
        out_specs=(P(None, "gz", "gx", "gy"), P(None, ("gx", "gy", "gz"), None)),
        check_vma=False,
    )
```

```python
import functools

import jax
import jax.numpy as jnp
from jax import lax
from jax.experimental import pallas as pl
from jax.experimental.pallas import tpu as pltpu
from jax.sharding import PartitionSpec as P

PATCH_DEV = 4
PS = 16
REFINE = 4
FP = 64
LANES = 128
MESH = pl.DeviceIdType.MESH

wave_ratio = 0.075
flux_ratio = 0.05
uplift_rate = 1.0
gravity = 1.0


def log2(n):
    assert n & (n - 1) == 0
    return n.bit_length() - 1


def iota(shape, dim):
    return lax.broadcasted_iota(jnp.int32, shape, dim)


def exact_dot(a, b):
    return jnp.dot(a, b, precision=lax.Precision.HIGHEST, preferred_element_type=jnp.float32)


def pick_sum(mask, values):
    picked = jnp.where(mask, values.astype(jnp.float32), 0.0)
    return jnp.sum(picked, axis=1, keepdims=True).astype(jnp.int32)


def six_neighbours(ext, yl, yr, f, z, z_index, rows, row0, depth):
    lane = iota((rows, LANES), 1)
    at = f * depth + z
    top = row0 + 8
    mid = ext[f, z_index, top : top + rows, :]
    left = jnp.where(
        lane == 0,
        pltpu.roll(yl[row0 : row0 + rows, :], (LANES - at) & (LANES - 1), 1),
        pltpu.roll(mid, 1, 1),
    )
    right = jnp.where(
        lane == LANES - 1,
        pltpu.roll(yr[row0 : row0 + rows, :], LANES - 1 - at, 1),
        pltpu.roll(mid, LANES - 1, 1),
    )
    return (
        ext[f, z_index + 1, top : top + rows, :],
        ext[f, z_index - 1, top : top + rows, :],
        ext[f, z_index, top + 1 : top + 1 + rows, :],
        ext[f, z_index, top - 1 : top - 1 + rows, :],
        right,
        left,
    )


def mean_of(six):
    return (six[0] + six[1] + six[2] + six[3] + six[4] + six[5]) * (1.0 / 6.0)


def neighbour_terms(part):
    height, flow_x, flow_y = part
    speed_x, speed_y = flow_x / height, flow_y / height
    head = 0.5 * gravity * height * height
    flux_x = [flow_x, flow_x * speed_x + head, flow_y * speed_x]
    flux_y = [flow_y, flow_x * speed_y, flow_y * speed_y + head]
    return [
        [0.25 * u + sign * flux_ratio * f for u, f in zip(part, flux)]
        for flux in (flux_x, flux_y)
        for sign in (1.0, -1.0)
    ]


def kernel(
    sizes,
    own_hbm, til_hbm, h_hbm, fl_hbm, vol_hbm, mat_hbm,
    outv, base_out, delta_out, coarse_out,
    state_in, ext, mat, ys_lo, ys_hi, yl, yr, strips, slots, lifts,
    own_ref, til_ref, vol_sem, mat_sem, in_sem, halo_send, halo_recv, st_send, st_recv, sib_send, sib_recv,
    lift_send, lift_recv,
):
    ngx, ngy, ngz, patches, depth, cx = sizes
    ndev = ngx * ngy * ngz
    nblk = ngx * ngy
    gx, gy, gz = lax.axis_index("gx"), lax.axis_index("gy"), lax.axis_index("gz")
    blk = gx * ngy + gy
    me = blk * ngz + gz
    local_x, local_y = cx // PS, LANES // PS
    tiles_x, tiles_y = local_x * ngx, local_y * ngy

    def coords(d):
        return (d // (ngy * ngz), (d // ngz) % ngy, d % ngz)

    vol_copies = [
        pltpu.make_async_copy(
            vol_hbm.at[f], ext.at[f, pl.ds(1, depth), pl.ds(8, cx), :], vol_sem.at[f]
        )
        for f in range(9)
    ]
    ins = [
        pltpu.make_async_copy(h_hbm, state_in.at[0], in_sem.at[0]),
        pltpu.make_async_copy(fl_hbm, state_in.at[pl.ds(1, 2)], in_sem.at[1]),
        pltpu.make_async_copy(own_hbm, own_ref, in_sem.at[2]),
        pltpu.make_async_copy(til_hbm, til_ref, in_sem.at[3]),
    ]
    for copy in ins:
        copy.start()
    for copy in vol_copies:
        copy.start()
    mat_copy = pltpu.make_async_copy(mat_hbm, mat, mat_sem)
    mat_copy.start()

    barrier = pltpu.get_barrier_semaphore()

    def greet(i, carry):
        pl.semaphore_signal(
            barrier, inc=1, device_id=coords((me + i) % ndev), device_id_type=MESH
        )
        return carry

    lax.fori_loop(1, ndev, greet, 0)

    @pl.when(gz == 0)
    def _():
        ext[:, 0] = jnp.zeros_like(ext[:, 0])

    @pl.when(gz == ngz - 1)
    def _():
        ext[:, depth + 1] = jnp.zeros_like(ext[:, depth + 1])

    @pl.when(gx == 0)
    def _():
        ext[:, 1 : depth + 1, 7:8, :] = jnp.zeros((9, depth, 1, LANES), jnp.float32)

    @pl.when(gx == ngx - 1)
    def _():
        ext[:, 1 : depth + 1, cx + 8 : cx + 9, :] = jnp.zeros((9, depth, 1, LANES), jnp.float32)

    @pl.when(gy == 0)
    def _():
        yl[...] = jnp.zeros_like(yl)

    @pl.when(gy == ngy - 1)
    def _():
        yr[...] = jnp.zeros_like(yr)

    lane4 = iota((PATCH_DEV, LANES), 1)
    half = lane4 & (FP - 1)
    for copy in ins:
        copy.wait()
    state = [state_in[0], state_in[1], state_in[2]]
    groups = FP * FP // LANES
    rows_own, cols_own = [], []
    for c in range(3):
        st = state[c]
        rows_own.append(jnp.where(lane4 < FP, st[:, :LANES], st[:, FP * FP - LANES :]))
        strips[gz, blk, 4 * c : 4 * c + 4, :] = rows_own[c]
        packed = jnp.zeros((PATCH_DEV, LANES), jnp.float32)
        for k in range(groups):
            part = st[:, LANES * k : LANES * (k + 1)]
            first = part if k == 0 else pltpu.roll(part, k, 1)
            packed = jnp.where(half == k, first, packed)
            packed = jnp.where(half == 32 + k, pltpu.roll(part, (k + 97) % LANES, 1), packed)
        cols_own.append(packed)
        strips[gz, blk, 12 + 4 * c : 16 + 4 * c, :] = packed

    lane_w = iota((PATCH_DEV, FP * FP), 1)
    col_w = lane_w & (FP - 1)
    span = FP * FP
    terms = neighbour_terms(state)
    moves = [
        (lane_w < FP, FP),
        (lane_w >= span - FP, span - FP),
        (col_w == 0, 1),
        (col_w == FP - 1, span - 1),
    ]
    for c in range(3):
        moved = [
            jnp.where(edge, terms[side][c], pltpu.roll(terms[side][c], shift, 1))
            for side, (edge, shift) in enumerate(moves)
        ]
        base_out[c] = (moved[0] + moved[1]) + (moved[2] + moved[3])

    for copy in vol_copies:
        copy.wait()

    lane_c = iota((cx, LANES), 1)

    def pack(z, carry):
        lo, hi = carry
        for f in range(9):
            at = f * depth + z
            u = ext[f, z + 1, 8 : 8 + cx, :]
            lo = jnp.where(lane_c == at, pltpu.roll(u, at, 1), lo)
            hi = jnp.where(lane_c == at, pltpu.roll(u, at + 1, 1), hi)
        return lo, hi

    zero_face = jnp.zeros((cx, LANES), jnp.float32)
    lo, hi = lax.fori_loop(0, depth, pack, (zero_face, zero_face))
    ys_lo[...] = lo
    ys_hi[...] = hi

    pl.semaphore_wait(barrier, ndev - 1)

    def remote(src, dst, k, target):
        return pltpu.make_async_remote_copy(
            src_ref=src, dst_ref=dst, send_sem=halo_send.at[k], recv_sem=halo_recv.at[k],
            device_id=target, device_id_type=MESH,
        )

    inner = pl.ds(1, depth)
    halos = [
        (gy < ngy - 1, gy > 0, remote(ys_hi, yl, 0, (gx, gy + 1, gz))),
        (gy > 0, gy < ngy - 1, remote(ys_lo, yr, 1, (gx, gy - 1, gz))),
        (gx < ngx - 1, gx > 0, remote(
            ext.at[:, inner, pl.ds(cx + 7, 1), :], ext.at[:, inner, pl.ds(7, 1), :],
            2, (gx + 1, gy, gz))),
        (gx > 0, gx < ngx - 1, remote(
            ext.at[:, inner, pl.ds(8, 1), :], ext.at[:, inner, pl.ds(cx + 8, 1), :],
            3, (gx - 1, gy, gz))),
        (gz < ngz - 1, gz > 0, remote(
            ext.at[:, depth, pl.ds(8, cx), :], ext.at[:, 0, pl.ds(8, cx), :],
            4, (gx, gy, gz + 1))),
        (gz > 0, gz < ngz - 1, remote(
            ext.at[:, 1, pl.ds(8, cx), :], ext.at[:, depth + 1, pl.ds(8, cx), :],
            5, (gx, gy, gz - 1))),
    ]
    for has_target, _, copy in halos:
        pl.when(has_target)(copy.start)

    def spread(i, carry):
        b = (blk + i) % nblk
        pltpu.make_async_remote_copy(
            src_ref=strips.at[gz, blk], dst_ref=strips.at[gz, blk],
            send_sem=st_send, recv_sem=st_recv,
            device_id=(b // ngy, b % ngy, gz), device_id_type=MESH,
        ).start()
        return carry

    lax.fori_loop(1, nblk, spread, 0)

    owner = own_ref[...]
    tile = til_ref[...]
    square = (patches, patches)
    owner_wide = jnp.broadcast_to(owner, square)
    owner_col = pick_sum(iota(square, 0) == iota(square, 1), owner_wide)
    earlier = (owner_col == owner_wide) & (iota(square, 0) < iota(square, 1))
    rank = jnp.sum(jnp.where(earlier, 1.0, 0.0), axis=0, keepdims=True).astype(jnp.int32)
    row_of = owner * PATCH_DEV + rank
    tile_x = tile >> log2(tiles_y)
    tile_y = tile & (tiles_y - 1)
    wide8 = (8, patches)
    row_of8 = jnp.broadcast_to(row_of, wide8)
    tile8 = jnp.broadcast_to(tile, wide8)
    mine = row_of8 == me * PATCH_DEV + iota(wide8, 0)
    mine = mine & (iota(wide8, 0) < PATCH_DEV)
    my_tile = pick_sum(mine, tile8)
    my_x = my_tile >> log2(tiles_y)
    my_y = my_tile & (tiles_y - 1)
    my_blk = (my_x >> log2(local_x)) * ngy + (my_y >> log2(local_y))

    founds, picks = [], []
    keys = (8, ndev * 24)
    for side, (valid, want) in enumerate(
        [
            (my_x > 0, my_tile - tiles_y),
            (my_x < tiles_x - 1, my_tile + tiles_y),
            (my_y > 0, my_tile - 1),
            (my_y < tiles_y - 1, my_tile + 1),
        ]
    ):
        match = tile8 == jnp.where(valid, want, -1)
        other = pick_sum(match, row_of8 + 1) - 1
        founds.append((other >= 0)[:PATCH_DEV])
        dev = other >> log2(PATCH_DEV)
        place = (dev & (ngz - 1)) * nblk + (dev >> log2(ngz))
        target = place * 24 + (other & (PATCH_DEV - 1))
        for c in range(3):
            q = c if side < 2 else 3 + c
            goal = jnp.where(other >= 0, target + 4 * q, -1)
            picks.append(jnp.where(iota(keys, 1) == goal, 1.0, 0.0))
    pick_all = jnp.concatenate(picks, axis=0)

    chooser = jnp.where(iota((8, nblk), 1) == my_blk, 1.0, 0.0)
    here = (tile_x >> log2(local_x) == gx) & (tile_y >> log2(local_y) == gy)
    here_wide = jnp.broadcast_to(jnp.where(here, 1, 0), square)
    here_col = pick_sum(iota(square, 0) == iota(square, 1), here_wide)
    before = (here_col == 1) & (iota(square, 0) < iota(square, 1))
    place_row = jnp.sum(jnp.where(before, 1.0, 0.0), axis=0, keepdims=True).astype(jnp.int32)
    place_row = jnp.where(here, place_row, -1)
    count = PATCH_DEV * ngz
    tall = (count * PS, patches)
    chosen = jnp.broadcast_to(place_row, tall) == (iota(tall, 0) >> log2(PS))
    local = (tile_x & (local_x - 1)) * local_y + (tile_y & (local_y - 1)) + 1
    local_col = pick_sum(chosen, jnp.broadcast_to(local, tall)) - 1
    local_tx = local_col >> log2(local_y)
    local_ty = local_col & (local_y - 1)
    row_want = local_tx * PS + (iota((count * PS, 1), 0) & (PS - 1))
    row_pick = jnp.where(iota((count * PS, cx), 1) == row_want, 1.0, 0.0)
    full = (count * PS, LANES)
    lane_pick = (iota(full, 1) >> log2(PS)) == local_ty
    owner_here = jnp.where(here, owner, -1)
    slot_wide = (2 * ndev, patches)
    owned = jnp.broadcast_to(owner_here, slot_wide) == (iota(slot_wide, 0) >> 1)
    slot_place = pick_sum(owned, jnp.broadcast_to(place_row + 1, slot_wide)) - 1
    slot_row = jnp.where(slot_place >= 0, 2 * slot_place + (iota((2 * ndev, 1), 0) & 1), -1)
    slot_pick = jnp.where(iota((2 * ndev, 2 * count), 1) == slot_row, 1.0, 0.0)

    for k in range(4):
        pl.when(halos[k][1])(halos[k][2].wait_recv)
    mat_copy.wait()

    @pl.when(gz == 0)
    def _():
        def six(f):
            return six_neighbours(ext, yl, yr, f, 0, 1, cx, 0, depth)

        vz = six(2)
        sxz, syz = six(7), six(8)
        szz = ext[5, 2, 8 : 8 + cx, :] - ext[5, 0, 8 : 8 + cx, :]
        rate = mat[0, 0] * ((sxz[2] - sxz[3]) + (syz[4] - syz[5]) + szz)
        floor = mean_of(vz) + wave_ratio * rate
        band = jnp.where(lane_pick, exact_dot(row_pick, floor), 0.0)
        same = (iota((LANES, LANES), 0) & (PS - 1)) == (iota((LANES, LANES), 1) & (PS - 1))
        spread_lanes = exact_dot(band, jnp.where(same, 1.0, 0.0))
        kept = jnp.where(
            (iota(full, 1) >> log2(PS)) == (iota(full, 0) & 7), spread_lanes, 0.0
        )
        rows = exact_dot(slot_pick, jnp.sum(kept.reshape(count * 2, 8, LANES), axis=1))
        for d in range(ndev):
            slots[d] = rows[2 * d : 2 * d + 2, :]

        def send_lift(i, carry):
            d = (me + i) % ndev
            pltpu.make_async_remote_copy(
                src_ref=slots.at[d], dst_ref=lifts.at[blk],
                send_sem=lift_send, recv_sem=lift_recv,
                device_id=coords(d), device_id_type=MESH,
            ).start()
            return carry

        lax.fori_loop(1, ndev, send_lift, 0)
        lifts[blk] = slots[me]

    for k in range(4, 6):
        pl.when(halos[k][1])(halos[k][2].wait_recv)

    def layer(z, carry):
        for row0 in range(0, cx, 16):
            sixes = {}

            def six(f):
                if f not in sixes:
                    sixes[f] = six_neighbours(ext, yl, yr, f, z, z + 1, 16, row0, depth)
                return sixes[f]

            def across(f, along):
                return six(f)[2 * along] - six(f)[2 * along + 1]

            def put(f, rate):
                outv[f, z, row0 : row0 + 16, :] = mean_of(six(f)) + wave_ratio * rate

            buoyancy = mat[0, z, row0 : row0 + 16, :]
            lame = mat[1, z, row0 : row0 + 16, :]
            shear = mat[2, z, row0 : row0 + 16, :]
            dx, dy, dz = across(0, 1), across(1, 2), across(2, 0)
            ldiv = lame * (dx + dy + dz)
            put(0, buoyancy * (across(3, 1) + across(6, 2) + across(7, 0)))
            put(1, buoyancy * (across(6, 1) + across(4, 2) + across(8, 0)))
            put(2, buoyancy * (across(7, 1) + across(8, 2) + across(5, 0)))
            put(3, ldiv + 2.0 * shear * dx)
            put(4, ldiv + 2.0 * shear * dy)
            put(5, ldiv + 2.0 * shear * dz)
            put(6, shear * (across(0, 2) + across(1, 1)))
            put(7, shear * (across(0, 0) + across(2, 1)))
            put(8, shear * (across(1, 0) + across(2, 2)))
        return carry

    first_part = depth // 2
    lax.fori_loop(0, first_part, layer, 0)

    some = strips.at[gz, pl.ds(0, nblk - 1)]
    pltpu.make_async_copy(some, some, st_recv).wait()

    def hand(i):
        other = (gz + i) % ngz
        return pltpu.make_async_remote_copy(
            src_ref=strips.at[gz], dst_ref=strips.at[gz],
            send_sem=sib_send.at[i - 1], recv_sem=sib_recv.at[i - 1],
            device_id=(gx, gy, other), device_id_type=MESH,
        )

    for i in range(1, ngz):
        hand(i).start()
    lax.fori_loop(first_part, depth, layer, 0)

    for i in range(1, ngz):
        hand(i).wait_recv()
    ghosts = exact_dot(pick_all, strips[...].reshape(ndev * 24, LANES))

    changes = []
    for side, (own, shift) in enumerate(
        [(rows_own, FP), (rows_own, FP), (cols_own, 96), (cols_own, 32)]
    ):
        part = [
            jnp.where(
                founds[side],
                pltpu.roll(ghosts[at : at + PATCH_DEV, :], shift, 1),
                own[c],
            )
            for c, at in enumerate(range(side * 24, side * 24 + 24, 8))
        ]
        new, old = neighbour_terms(part)[side], neighbour_terms(own)[side]
        changes.append([new[c] - old[c] for c in range(3)])
    for c in range(3):
        delta_out[c, :PATCH_DEV, :] = jnp.where(lane4 < FP, changes[0][c], changes[1][c])
        delta_out[3 + c, :PATCH_DEV, :] = jnp.where(half < 32, changes[2][c], changes[3][c])

    @pl.when(gz == 0)
    def _():
        part = lifts.at[pl.ds(0, nblk - 1)]
        pltpu.make_async_copy(part, part, lift_recv).wait()

    @pl.when(gz != 0)
    def _():
        pltpu.make_async_copy(lifts, lifts, lift_recv).wait()

    for k in range(2):
        coarse_out[8 * k : 8 * k + 8, :] = exact_dot(chooser, lifts[:, k, :])

    for has_target, _, copy in halos:
        pl.when(has_target)(copy.wait_send)
    pltpu.make_async_copy(some, some, st_send).wait()
    for i in range(1, ngz):
        hand(i).wait_send()

    @pl.when(gz == 0)
    def _():
        sent = slots.at[pl.ds(0, ndev - 1)]
        pltpu.make_async_copy(sent, sent, lift_send).wait()


def finish(outv, base_ref, delta_ref, coarse_ref, vout_hbm, wout_ref, out_sem):
    stores = [
        pltpu.make_async_copy(outv.at[f], vout_hbm.at[f], out_sem.at[f]) for f in range(9)
    ]
    for store in stores:
        store.start()
    groups = FP * FP // LANES
    wide_lane = iota((LANES, 8 * LANES), 1)
    source = (wide_lane >> log2(LANES)) * PS + ((wide_lane & (FP - 1)) >> log2(REFINE))
    expand = jnp.where(iota((LANES, 8 * LANES), 0) == source, 1.0, 0.0)
    fine = exact_dot(coarse_ref[...], expand)
    lane4 = iota((PATCH_DEV, LANES), 1)
    half = lane4 & (FP - 1)
    for c in range(3):
        rows = delta_ref[c, :PATCH_DEV, :]
        cols = delta_ref[3 + c, :PATCH_DEV, :]
        for k in range(groups):
            at = pl.ds(LANES * k, LANES)
            value = base_ref[c, :, at]
            low = cols if k == 0 else pltpu.roll(cols, LANES - k, 1)
            high = cols if k == 31 else pltpu.roll(cols, (31 - k) % LANES, 1)
            value = value + jnp.where(half == 0, low, jnp.where(half == FP - 1, high, 0.0))
            if k == 0:
                value = value + jnp.where(lane4 < FP, rows, 0.0)
            if k == groups - 1:
                value = value + jnp.where(lane4 < FP, 0.0, rows)
            if c == 0:
                r = k // 2
                top = 8 * (r // 8)
                lift = fine[top : top + PATCH_DEV, LANES * (r % 8) : LANES * (r % 8 + 1)]
                value = value + uplift_rate * lift
            wout_ref[c, :, at] = value
    for store in stores:
        store.wait()


def per_device(volume, materials, water_height, water_flow, owner_of, patch_tile):
    ngx, ngy, ngz = (lax.axis_size(a) for a in ("gx", "gy", "gz"))
    ndev, nblk = ngx * ngy * ngz, ngx * ngy
    fields, depth, cx, cy = volume.shape
    patches = owner_of.shape[0]
    assert cy == LANES and fields * depth <= LANES
    f32 = jnp.float32
    dma = pltpu.SemaphoreType.DMA
    vmem = pl.BlockSpec(memory_space=pltpu.VMEM)
    hbm = pl.BlockSpec(memory_space=pltpu.HBM)
    whole = functools.partial(pltpu.with_memory_space_constraint, memory_space=pltpu.VMEM)
    middle = pl.pallas_call(
        functools.partial(kernel, (ngx, ngy, ngz, patches, depth, cx)),
        name="coupled_step",
        out_shape=(
            pltpu.VMEM(volume.shape, f32),
            pltpu.VMEM((3,) + water_height.shape, f32),
            pltpu.VMEM((6, 8, LANES), f32),
            pltpu.VMEM((16, LANES), f32),
        ),
        in_specs=[hbm] * 6,
        out_specs=(vmem,) * 4,
        scratch_shapes=[
            pltpu.VMEM((3,) + water_height.shape, f32),
            pltpu.VMEM((fields, depth + 2, cx + 16, LANES), f32),
            pltpu.VMEM(materials.shape, f32),
            pltpu.VMEM((cx, LANES), f32),
            pltpu.VMEM((cx, LANES), f32),
            pltpu.VMEM((cx, LANES), f32),
            pltpu.VMEM((cx, LANES), f32),
            pltpu.VMEM((ngz, nblk, 24, LANES), f32),
            pltpu.VMEM((ndev, 2, LANES), f32),
            pltpu.VMEM((nblk, 2, LANES), f32),
            pltpu.VMEM((1, patches), jnp.int32), pltpu.VMEM((1, patches), jnp.int32),
            dma((fields,)), dma, dma((4,)), dma((6,)), dma((6,)), dma, dma,
            dma((max(ngz - 1, 1),)), dma((max(ngz - 1, 1),)), dma, dma,
        ],
        compiler_params=pltpu.CompilerParams(
            collective_id=0, has_side_effects=True, vmem_limit_bytes=40 * 1024 * 1024
        ),
    )(
        *[
            pltpu.with_memory_space_constraint(part, pltpu.HBM)
            for part in (
                owner_of.reshape(1, patches), patch_tile.reshape(1, patches),
                water_height, water_flow, volume, materials,
            )
        ]
    )
    middle = [whole(part) for part in middle]
    return pl.pallas_call(
        finish,
        name="finish_step",
        out_shape=(
            jax.ShapeDtypeStruct(volume.shape, f32),
            jax.ShapeDtypeStruct((3,) + water_height.shape, f32),
        ),
        in_specs=[vmem] * 4,
        out_specs=(hbm, vmem),
        scratch_shapes=[dma((fields,))],
        compiler_params=pltpu.CompilerParams(vmem_limit_bytes=16 * 1024 * 1024),
    )(*middle)


def solution(mesh):
    return jax.shard_map(
        per_device,
        mesh=mesh,
        in_specs=(
            P(None, "gz", "gx", "gy"),
            P(None, "gz", "gx", "gy"),
            P(("gx", "gy", "gz"), None),
            P(None, ("gx", "gy", "gz"), None),
            P(),
            P(),
        ),
        out_specs=(P(None, "gz", "gx", "gy"), P(None, ("gx", "gy", "gz"), None)),
        check_vma=False,
    )
```
